768 devices in a mesh: ctx: 96 (over z, x, core), head: 8 (over y).
Axes of the slice: x: 4, y: 8, z: 12, core: 2. Of those that a mesh axis runs over, the one named last changes fastest.
Arguments:
- queries: float32 [2, 12288, 2048], P(None, 'ctx', 'head'), may hold values from -6 to 6
- keys: float32 [12288, 2048], P('ctx', 'head'), may hold values from -6 to 6
- values: float32 [12288, 2048], P('ctx', 'head'), may hold values from -6 to 6
- rates: float32 [12288, 8], P('ctx', 'head'), may hold values from 0.02 to 0.2
- grad_out: float32 [2, 12288, 2048], P(None, 'ctx', 'head'), may hold values from -6 to 6
- w_gate: float32 [8, 256, 512], P('head'), may hold values from -0.375 to 0.375
- w_up: float32 [8, 256, 512], P('head'), may hold values from -0.375 to 0.375
- w_down: float32 [8, 512, 256], P('head'), may hold values from -0.25 to 0.25
Outputs:
- grad_queries: float32 [2, 12288, 2048], P(None, 'ctx', 'head')
- grad_keys: float32 [12288, 2048], P('ctx', 'head')
- grad_values: float32 [12288, 2048], P('ctx', 'head')
The draws below stay inside these ranges and needn't reach their ends.
All inputs are finite; a program needn't handle non-finite values.
Results may differ from the reference program's by a relative error of at most 0.00013.
Values sent between devices are 32-bit elements; how exact they have to be, the bound alone decides.
No kernel may reach another device: no remote copies, remote signals or barrier semaphores. Data moves between devices by JAX's collectives and lax.ppermute only.
A program may use at most 32 MiB of HBM per device.

```python
import math
import jax
import jax.numpy as jnp
from jax import lax

HD = 256
FH = 512
HEADS = 8
GROUP = 12288


def steps_of(stream_key, dims, shards, low, top_value):
    gain = 1.0
    for axis_at, shards_of in shards:
        heights = jax.random.uniform(jax.random.fold_in(jax.random.fold_in(stream_key, 6), axis_at), (shards_of,), jnp.float32, low / len(shards), top_value / len(shards))
        gain = gain * jnp.repeat(jnp.exp(heights), dims[axis_at] // shards_of).reshape((-1,) + (1,) * (len(dims) - 1 - axis_at))
    return gain


def centred(key, shape, scale, bound, shards=(), kind=jnp.bfloat16):
    array = jax.random.normal(key, shape, jnp.float32) * scale
    if len(shards) > 0:
        array = steps_of(key, shape, shards, -0.22, 0.18) * array
    return jnp.clip(array, min=-bound, max=bound).astype(kind)


def setup_inputs(seed: int = 0) -> dict:
    streams_of = jax.random.split(jax.random.key(seed), 9)
    return {
        "queries": centred(streams_of[0], (2, GROUP, HEADS * HD), 1.0, 6.0, ((1, 96), (2, 8)), jnp.float32),
        "keys": centred(streams_of[1], (GROUP, HEADS * HD), 1.0, 6.0, ((0, 96), (1, 8)), jnp.float32),
        "values": centred(streams_of[2], (GROUP, HEADS * HD), 1.0, 6.0, ((0, 96), (1, 8)), jnp.float32),
        "rates": jnp.clip(jnp.exp(math.log(0.2) - 2.3025851 * jax.random.uniform(streams_of[3], (GROUP, HEADS), jnp.float32) ** steps_of(streams_of[3], (GROUP, HEADS), ((0, 96), (1, 8)), -0.2, 0.2)), 0.02, 0.2),
        "grad_out": centred(streams_of[4], (2, GROUP, HEADS * HD), 1.0, 6.0, ((1, 96), (2, 8)), jnp.float32),
        "w_gate": centred(streams_of[5], (HEADS, HD, FH), HD ** -0.5, 0.375, ((0, 8),), jnp.float32),
        "w_up": centred(streams_of[6], (HEADS, HD, FH), HD ** -0.5, 0.375, ((0, 8),), jnp.float32),
        "w_down": centred(streams_of[7], (HEADS, FH, HD), FH ** -0.5, 0.25, ((0, 8),), jnp.float32),
    }


def apply_fast(weights, inputs):
    w_gate, w_up, w_down = weights
    best = lax.Precision.HIGHEST
    gate = jnp.dot(inputs, w_gate, precision=best)
    up_part = jnp.dot(inputs, w_up, precision=best)
    return jnp.dot(jax.nn.silu(gate) * up_part, w_down, precision=best)

def inner_score(weights, keys_head, values_head, rates_head):
    return jnp.sum(rates_head[:, None] * apply_fast(weights, keys_head) * values_head)

def head_backward(packed):
    query_zero, query_one, keys_head, values_head, rates_head, cot_zero, cot_one, w_gate, w_up, w_down = packed
    scale = GROUP ** (-0.5)
    initial = (w_gate, w_up, w_down)
    inner = jax.grad(inner_score)(initial, keys_head, values_head, rates_head)
    updated = tuple((w + scale * g for w, g in zip(initial, inner)))
    pull_zero = jax.vjp(lambda y: apply_fast(initial, y), query_zero)[1]
    grad_zero = pull_zero(cot_zero)[0]
    pull_one = jax.vjp(apply_fast, updated, query_one)[1]
    direction, grad_one = pull_one(cot_one)

    def coupled(key_rows, value_rows):
        tangent = jax.jvp(lambda ww: inner_score(ww, key_rows, value_rows, rates_head), (initial,), (direction,))[1]
        return scale * tangent
    grad_key, grad_value = jax.grad(coupled, argnums=(0, 1))(keys_head, values_head)
    return (grad_zero, grad_one, grad_key, grad_value)

def reference(queries, keys, values, rates, grad_out, w_gate, w_up, w_down):
    per_query = queries.reshape(2, GROUP, HEADS, HD).transpose(2, 0, 1, 3)
    per_cot = grad_out.reshape(2, GROUP, HEADS, HD).transpose(2, 0, 1, 3)
    per_key = keys.reshape(GROUP, HEADS, HD).transpose(1, 0, 2)
    per_value = values.reshape(GROUP, HEADS, HD).transpose(1, 0, 2)
    per_rate = rates.T
    grad_zero, grad_one, grad_key, grad_value = lax.map(head_backward, (per_query[:, 0], per_query[:, 1], per_key, per_value, per_rate, per_cot[:, 0], per_cot[:, 1], w_gate, w_up, w_down))
    grad_queries = jnp.stack([grad_zero, grad_one], axis=1).transpose(1, 2, 0, 3).reshape(2, GROUP, HEADS * HD)
    grad_keys = grad_key.transpose(1, 0, 2).reshape(GROUP, HEADS * HD)
    grad_values = grad_value.transpose(1, 0, 2).reshape(GROUP, HEADS * HD)
    return (grad_queries, grad_keys, grad_values)
```

```python
import functools

import jax
import jax.numpy as jnp
from jax import lax
from jax.experimental import pallas as pl
from jax.experimental.pallas import tpu as pltpu
from jax.sharding import Mesh
from jax.sharding import PartitionSpec as P

NX, NC = 4, 2
NN = ((1,), (0,))
NT = ((1,), (1,))
MIB = 1 << 20
LANES = 128


def split(a):
    head = a.astype(jnp.bfloat16)
    tail = (a - head.astype(jnp.float32)).astype(jnp.bfloat16)
    return head, tail


def dot3(a, b, dims):
    rows = a[0].shape[0]
    dot = functools.partial(
        lax.dot_general, dimension_numbers=(dims, ((), ())), preferred_element_type=jnp.float32
    )
    both = dot(jnp.concatenate(a, axis=0), b[0])
    return both[:rows] + (both[rows:] + dot(a[0], b[1]))


def gates(gate):
    sigma = jax.nn.sigmoid(gate)
    return sigma, gate * sigma, sigma * (1.0 + gate * (1.0 - sigma))


def call(kernel, shapes, flops, n_bytes, limit=16, **more):
    return pl.pallas_call(
        kernel,
        out_shape=shapes,
        **more,
        compiler_params=pltpu.CompilerParams(vmem_limit_bytes=limit * MIB),
        cost_estimate=pl.CostEstimate(flops=flops, bytes_accessed=n_bytes, transcendentals=0),
    )


def start_all(pairs, sems):
    copies = [pltpu.make_async_copy(*pair, sems.at[i]) for i, pair in enumerate(pairs)]
    for copy in copies:
        copy.start()
    return copies


def pack_kernel(k_ref, v_ref, r_ref, inner_ref, rate_ref, raw_ref, row_ref, sems):
    width = k_ref.shape[1]
    tok = r_ref.shape[1]
    copies = start_all([(r_ref, row_ref), (v_ref, raw_ref), (k_ref, inner_ref.at[:, :width])], sems)
    copies[0].wait()
    rate = jnp.broadcast_to(row_ref[...], (LANES, tok)).T
    rate_ref[...] = rate
    copies[1].wait()
    for at in range(0, width, LANES):
        inner_ref[:, width + at : width + at + LANES] = rate * raw_ref[:, at : at + LANES]
    copies[2].wait()


def units_kernel(wg_ref, wu_ref, wd_ref, q_ref, c_ref, out_ref, ask_ref, raw_ref, sems):
    nx, rows, width = out_ref.shape
    units = rows // 3
    half = nx * units
    start = pl.multiple_of(lax.axis_index("c") * half, LANES)
    pairs = [
        (wg_ref.at[0, :, pl.ds(start, half)], raw_ref.at[0]),
        (wu_ref.at[0, :, pl.ds(start, half)], raw_ref.at[1]),
    ]
    pairs += [(wd_ref.at[0, pl.ds(start + i * units, units)], out_ref.at[i, 2 * units :]) for i in range(nx)]
    tok = q_ref.shape[1]
    copies = start_all(pairs + [(q_ref.at[1], ask_ref.at[:tok]), (c_ref.at[1], ask_ref.at[tok:])], sems)
    for i in range(2):
        copies[i].wait()
        out_ref[:, i * units : (i + 1) * units] = raw_ref[i].T.reshape(nx, units, width)
    for copy in copies[2:]:
        copy.wait()


def row_sum_kernel(in_ref, out_ref, ask_ref):
    nx = in_ref.shape[0]
    rows = out_ref.shape[0]
    tok = ask_ref.shape[1] // nx
    total = in_ref[0, :rows]
    for i in range(1, nx):
        total += in_ref[i, :rows]
    out_ref[...] = total
    for i in range(nx):
        for j in range(2):
            ask_ref[j, i * tok : (i + 1) * tok] = in_ref[i, rows + j * tok : rows + (j + 1) * tok]


def update_kernel(scale, in_ref, w_ref, out_ref):
    n = in_ref.shape[0]
    total = in_ref[0]
    for i in range(1, n):
        total += in_ref[i]
    total = w_ref[...] + scale * total
    for i in range(n):
        out_ref[i] = total


def total_kernel(in_ref, out_ref):
    n = in_ref.shape[0]
    total = in_ref[0]
    for i in range(1, n):
        total += in_ref[i]
    for i in range(n):
        out_ref[i] = total


def parts(ref, units):
    width = ref.shape[2]
    return [ref[:, i * units : (i + 1) * units].reshape(-1, width) for i in range(3)]


def weight_grad(w_in, w_down, chunks):
    n = w_down[0].shape[0]
    total = None
    for rows, cots in chunks:
        rows, cots = split(rows), split(cots)
        both = dot3(w_in, rows, NT)
        hidden_grad = dot3(w_down, cots, NT)
        up_part = both[n:]
        _, active, slope = gates(both[:n])
        in_grad = jnp.concatenate([hidden_grad * up_part * slope, hidden_grad * active], axis=0)
        new = dot3(split(in_grad), rows, NN), dot3(split(active * up_part), cots, NN)
        total = new if total is None else (total[0] + new[0], total[1] + new[1])
    return total


def inner_kernel(own_ref, other_ref, ask_ref, w_ref, out_ref, piece_ref, pair_ref, kept_ref, sems):
    nx, rows, width = w_ref.shape
    units = rows // 3
    n = nx * units
    tok = own_ref.shape[0]
    copies = start_all([(own_ref, pair_ref.at[:tok]), (other_ref, pair_ref.at[tok:]), (w_ref, kept_ref)], sems)
    piece = piece_ref.shape[0]
    start = pl.multiple_of(lax.axis_index("z") * piece, 8)
    piece_ref[...] = w_ref[lax.axis_index("x"), pl.ds(start, piece)]
    w_gate, w_up, w_down = parts(w_ref, units)
    pair = jnp.concatenate([own_ref[...], other_ref[...]], axis=0)
    in_sum, down_sum = weight_grad(
        split(jnp.concatenate([w_gate, w_up], axis=0)), split(w_down), [(pair[:, :width], pair[:, width:])]
    )
    out_ref[:, :units] = in_sum[:n].reshape(nx, units, width)
    out_ref[:, units : 2 * units] = in_sum[n:].reshape(nx, units, width)
    out_ref[:, 2 * units : rows] = down_sum.reshape(nx, units, width)
    for i in range(nx):
        out_ref[i, rows:] = ask_ref[...]
    for copy in copies:
        copy.wait()


def outer_kernel(ask_ref, got_ref, w_ref, out_ref, pair_ref, sems):
    width = w_ref.shape[1]
    units = w_ref.shape[0] // 3
    tok = pair_ref.shape[0] // 2
    at = pl.ds(pl.multiple_of(lax.axis_index("x") * tok, 8), tok)
    copies = start_all(
        [
            (ask_ref.at[0, at], pair_ref.at[:tok, :width]),
            (ask_ref.at[1, at], pair_ref.at[:tok, width:]),
            (got_ref.at[0, at], pair_ref.at[tok:, :width]),
            (got_ref.at[1, at], pair_ref.at[tok:, width:]),
        ],
        sems,
    )
    step = 256
    chunks = [
        (ref[0, at : at + step], ref[1, at : at + step])
        for ref in (ask_ref, got_ref)
        for at in range(0, ref.shape[1], step)
    ]
    in_sum, down_sum = weight_grad(split(w_ref[: 2 * units]), split(w_ref[2 * units :]), chunks)
    out_ref[: 2 * units] = in_sum
    out_ref[2 * units :] = down_sum
    for copy in copies:
        copy.wait()


def query_grad(rows, cots, w_gate, w_up, w_down, up_way, down_way):
    rows, cots = split(rows), split(cots)
    gate, up_part = dot3(rows, w_gate, up_way), dot3(rows, w_up, up_way)
    hidden_grad = dot3(cots, w_down, NT)
    _, active, slope = gates(gate)
    return dot3(split(hidden_grad * up_part * slope), w_gate, down_way) + dot3(
        split(hidden_grad * active), w_up, down_way
    )


def query_kernel(q_ref, c_ref, wg_ref, wu_ref, wd_ref, pair_ref, w_ref, zero_ref, mine_ref, theirs_ref):
    tok, width = zero_ref.shape
    zero_ref[...] = query_grad(
        q_ref[0], c_ref[0], split(wg_ref[0]), split(wu_ref[0]), split(wd_ref[0]), NN, NT
    )
    w_gate, w_up, w_down = [split(w) for w in parts(w_ref, w_ref.shape[1] // 3)]
    grad = query_grad(pair_ref[:, :width], pair_ref[:, width:], w_gate, w_up, w_down, NT, NN)
    mine_ref[...] = grad[:tok]
    theirs_ref[...] = grad[tok:]


def final_kernel(d_ref, pair_ref, w_ref, query_ref, mine_ref, theirs_ref):
    width = d_ref.shape[2]
    units = d_ref.shape[1] // 3
    w_gate, w_up, w_down = [split(w) for w in parts(w_ref, units)]
    rows, cots = split(pair_ref[:, :width]), split(pair_ref[:, width:])
    gate, up_part = dot3(rows, w_gate, NT), dot3(rows, w_up, NT)
    hidden_grad = dot3(cots, w_down, NT)
    sigma, active, slope = gates(gate)
    bend = sigma * (1.0 - sigma) * (2.0 + gate * (1.0 - 2.0 * sigma))
    steep = slope * up_part
    d_gate, d_up, d_down = [split(d) for d in parts(d_ref, units)]
    d_g, d_u = dot3(rows, d_gate, NT), dot3(rows, d_up, NT)
    d_c = dot3(cots, d_down, NT)
    d_h = steep * d_g + active * d_u
    value = dot3(split(active * up_part), d_down, NN) + dot3(split(d_h), w_down, NN)
    to_gate = hidden_grad * (up_part * bend * d_g + slope * d_u) + steep * d_c
    to_up = hidden_grad * slope * d_g + active * d_c
    key = (
        dot3(split(hidden_grad * steep), d_gate, NN)
        + dot3(split(hidden_grad * active), d_up, NN)
        + dot3(split(to_gate), w_gate, NN)
        + dot3(split(to_up), w_up, NN)
    )
    tok = mine_ref.shape[0]
    mine_ref[:, :width] = key[:tok]
    mine_ref[:, width:] = value[:tok]
    theirs_ref[:, :width] = key[tok:]
    theirs_ref[:, width : 2 * width] = value[tok:]
    theirs_ref[:, 2 * width :] = query_ref[...]


def join_kernel(scale, mine_ref, got_ref, rate_ref, zero_ref, one_ref, q_ref, k_ref, v_ref):
    width = k_ref.shape[1]
    q_ref[0] = zero_ref[...]
    q_ref[1] = one_ref[...] + got_ref[:, 2 * width :]
    k_ref[...] = scale * (mine_ref[:, :width] + got_ref[:, :width])
    rate = scale * rate_ref[...]
    for at in range(0, width, LANES):
        lanes = slice(width + at, width + at + LANES)
        v_ref[:, at : at + LANES] = rate * (mine_ref[:, lanes] + got_ref[:, lanes])


def after(value, *others):
    return lax.optimization_barrier((value, others))[0]


def both(*values):
    return lax.optimization_barrier(values)


def body(queries, keys, values, rates, grad_out, w_gate, w_up, w_down):
    tok, width = keys.shape
    hidden = w_gate.shape[2]
    n_z = lax.axis_size("z")
    units = hidden // (NX * NC)
    half = NX * units
    piece = 3 * units // n_z
    scale = float(tok * NX * NC * n_z) ** (-0.5)
    f32 = lambda *shape: jax.ShapeDtypeStruct(shape, jnp.float32)
    swap = lambda x: lax.ppermute(x, "c", [(i, (i + 1) % NC) for i in range(NC)])
    gather = lambda x: lax.all_gather(x, "x", axis=0, tiled=True)
    exchange = lambda x: lax.all_to_all(x.reshape(n_z, piece, width), "z", 0, 0)
    hold = lambda x: pltpu.with_memory_space_constraint(x, pltpu.HBM)
    n_mul = 2 * tok * width * half
    n_w = 12 * width * half
    here, there = pl.BlockSpec(memory_space=pltpu.VMEM), pl.BlockSpec(memory_space=pltpu.HBM)

    own, rate = call(
        pack_kernel,
        [f32(tok, 2 * width), f32(tok, LANES)],
        0,
        16 * tok * width,
        in_specs=[there] * 3,
        out_specs=[here] * 2,
        scratch_shapes=[
            pltpu.VMEM((tok, width), jnp.float32), pltpu.VMEM((1, tok), jnp.float32), pltpu.SemaphoreType.DMA((3,))
        ],
    )(hold(keys), hold(values), hold(rates.reshape(1, tok)))
    other = swap(own)
    w_rows, ask = call(
        units_kernel,
        [f32(NX, 3 * units, width), f32(2 * tok, width)],
        0,
        2 * n_w,
        in_specs=[there] * 5,
        out_specs=[here] * 2,
        scratch_shapes=[pltpu.VMEM((2, width, half), jnp.float32), pltpu.SemaphoreType.DMA((4 + NX,))],
    )(hold(w_gate), hold(w_up), hold(w_down), hold(queries), hold(grad_out))

    pair_shape = pltpu.HBM((2 * tok, 2 * width), jnp.float32)
    kept_shape = pltpu.HBM((NX, 3 * units, width), jnp.float32)
    inner, w_piece, pair, kept = call(
        inner_kernel,
        [f32(NX, 3 * units + 2 * tok, width), f32(piece, width), pair_shape, kept_shape],
        36 * n_mul,
        2 * n_w,
        in_specs=[here] * 4,
        out_specs=[here, here, there, there],
        scratch_shapes=[pltpu.SemaphoreType.DMA((3,))],
    )(own, other, ask, w_rows)
    inner = lax.all_to_all(inner, "x", 0, 0)
    inner, ask = call(row_sum_kernel, [f32(3 * units, width), f32(2, NX * tok, width)], 0, 4 * n_w)(inner)
    pieces = f32(n_z, piece, width)
    new = call(functools.partial(update_kernel, scale), pieces, 0, n_w)(exchange(inner), w_piece)
    ask_got = swap(after(ask, new))
    new, ask_got = both(exchange(new).reshape(3 * units, width), ask_got)

    outer, asked = call(
        outer_kernel,
        [f32(3 * units, width), pair_shape],
        36 * n_mul,
        64 * tok * width,
        in_specs=[here] * 3,
        out_specs=[here, there],
        scratch_shapes=[pltpu.SemaphoreType.DMA((4,))],
    )(ask, ask_got, new)
    got, new_x = both(exchange(outer), gather(after(new, outer)))
    outer = call(total_kernel, pieces, 0, n_w)(got)
    new_x = after(new_x, outer).reshape(NX, 3 * units, width)
    zero, one, one_theirs = call(query_kernel, [f32(tok, width)] * 3, 60 * n_mul, 4 * n_w)(
        queries, grad_out, w_gate, w_up, w_down, asked, new_x
    )
    outer, one_theirs = both(exchange(outer).reshape(3 * units, width), one_theirs)
    d_all = gather(outer).reshape(NX, 3 * units, width)
    mine, theirs = call(
        final_kernel, [f32(tok, 2 * width), f32(tok, 3 * width)], 72 * n_mul, 3 * n_w
    )(d_all, pair, kept, one_theirs)
    return call(
        functools.partial(join_kernel, scale), [f32(2, tok, width), f32(tok, width), f32(tok, width)], 0, 40 * tok * width
    )(mine, swap(theirs), rate, zero, one)


def solution(mesh):
    devices = mesh.devices.reshape(-1, NX, NC, mesh.devices.shape[1])
    fine = Mesh(devices, ("z", "x", "c", "head"))
    ctx = ("z", "x", "c")
    in_specs = (
        P(None, ctx, "head"),
        P(ctx, "head"),
        P(ctx, "head"),
        P(ctx, "head"),
        P(None, ctx, "head"),
        P("head", None, None),
        P("head", None, None),
        P("head", None, None),
    )
    out_specs = (P(None, ctx, "head"), P(ctx, "head"), P(ctx, "head"))
    return jax.shard_map(body, mesh=fine, in_specs=in_specs, out_specs=out_specs, check_vma=False)
```

```python
import functools

import jax
import jax.numpy as jnp
from jax import lax
from jax.experimental import pallas as pl
from jax.experimental.pallas import tpu as pltpu
from jax.sharding import Mesh
from jax.sharding import PartitionSpec as P

NX, NC = 4, 2
NN = ((1,), (0,))
NT = ((1,), (1,))
MIB = 1 << 20
LANES = 128


def split(a):
    head = a.astype(jnp.bfloat16)
    tail = (a - head.astype(jnp.float32)).astype(jnp.bfloat16)
    return head, tail


def dot3(a, b, dims):
    rows = a[0].shape[0]
    dot = functools.partial(
        lax.dot_general, dimension_numbers=(dims, ((), ())), preferred_element_type=jnp.float32
    )
    both = dot(jnp.concatenate(a, axis=0), b[0])
    return both[:rows] + (both[rows:] + dot(a[0], b[1]))


def gates(gate):
    sigma = jax.nn.sigmoid(gate)
    return sigma, gate * sigma, sigma * (1.0 + gate * (1.0 - sigma))


def call(kernel, shapes, flops, n_bytes, limit=16, **more):
    return pl.pallas_call(
        kernel,
        out_shape=shapes,
        **more,
        compiler_params=pltpu.CompilerParams(vmem_limit_bytes=limit * MIB),
        cost_estimate=pl.CostEstimate(flops=flops, bytes_accessed=n_bytes, transcendentals=0),
    )


def start_all(pairs, sems):
    copies = [pltpu.make_async_copy(*pair, sems.at[i]) for i, pair in enumerate(pairs)]
    for copy in copies:
        copy.start()
    return copies


def pack_kernel(k_ref, v_ref, r_ref, inner_ref, rate_ref, raw_ref, row_ref, sems):
    width = k_ref.shape[1]
    tok = r_ref.shape[1]
    copies = start_all([(r_ref, row_ref), (v_ref, raw_ref), (k_ref, inner_ref.at[:, :width])], sems)
    copies[0].wait()
    rate = jnp.broadcast_to(row_ref[...], (LANES, tok)).T
    rate_ref[...] = rate
    copies[1].wait()
    for at in range(0, width, LANES):
        inner_ref[:, width + at : width + at + LANES] = rate * raw_ref[:, at : at + LANES]
    copies[2].wait()


def units_kernel(wg_ref, wu_ref, wd_ref, out_ref, raw_ref, sems):
    nx, rows, width = out_ref.shape
    units = rows // 3
    half = nx * units
    start = pl.multiple_of(lax.axis_index("c") * half, LANES)
    pairs = [
        (wg_ref.at[0, :, pl.ds(start, half)], raw_ref.at[0]),
        (wu_ref.at[0, :, pl.ds(start, half)], raw_ref.at[1]),
    ]
    pairs += [(wd_ref.at[0, pl.ds(start + i * units, units)], out_ref.at[i, 2 * units :]) for i in range(nx)]
    copies = start_all(pairs, sems)
    for i in range(2):
        copies[i].wait()
        out_ref[:, i * units : (i + 1) * units] = raw_ref[i].T.reshape(nx, units, width)
    for copy in copies[2:]:
        copy.wait()


def row_sum_kernel(in_ref, out_ref):
    total = in_ref[0]
    for i in range(1, in_ref.shape[0]):
        total += in_ref[i]
    out_ref[...] = total


def update_kernel(scale, in_ref, w_ref, out_ref):
    n = in_ref.shape[0]
    total = in_ref[0]
    for i in range(1, n):
        total += in_ref[i]
    total = w_ref[...] + scale * total
    for i in range(n):
        out_ref[i] = total


def total_kernel(in_ref, out_ref):
    n = in_ref.shape[0]
    total = in_ref[0]
    for i in range(1, n):
        total += in_ref[i]
    for i in range(n):
        out_ref[i] = total


def parts(ref, units):
    width = ref.shape[2]
    return [ref[:, i * units : (i + 1) * units].reshape(-1, width) for i in range(3)]


def weight_grad(w_in, w_down, chunks):
    n = w_down[0].shape[0]
    total = None
    for rows, cots in chunks:
        rows, cots = split(rows), split(cots)
        both = dot3(w_in, rows, NT)
        hidden_grad = dot3(w_down, cots, NT)
        up_part = both[n:]
        _, active, slope = gates(both[:n])
        in_grad = jnp.concatenate([hidden_grad * up_part * slope, hidden_grad * active], axis=0)
        new = dot3(split(in_grad), rows, NN), dot3(split(active * up_part), cots, NN)
        total = new if total is None else (total[0] + new[0], total[1] + new[1])
    return total


def inner_kernel(own_ref, other_ref, w_ref, q_ref, c_ref, out_ref, piece_ref, ask_ref, pair_ref, kept_ref, sems):
    nx, rows, width = w_ref.shape
    units = rows // 3
    n = nx * units
    tok = own_ref.shape[0]
    pairs = [(q_ref.at[1], ask_ref.at[:, :width]), (c_ref.at[1], ask_ref.at[:, width:])]
    pairs += [(own_ref, pair_ref.at[:tok]), (other_ref, pair_ref.at[tok:]), (w_ref, kept_ref)]
    copies = start_all(pairs, sems)
    piece = piece_ref.shape[0]
    start = pl.multiple_of(lax.axis_index("z") * piece, 8)
    piece_ref[...] = w_ref[lax.axis_index("x"), pl.ds(start, piece)]
    w_gate, w_up, w_down = parts(w_ref, units)
    pair = jnp.concatenate([own_ref[...], other_ref[...]], axis=0)
    in_sum, down_sum = weight_grad(
        split(jnp.concatenate([w_gate, w_up], axis=0)), split(w_down), [(pair[:, :width], pair[:, width:])]
    )
    out_ref[:, :units] = in_sum[:n].reshape(nx, units, width)
    out_ref[:, units : 2 * units] = in_sum[n:].reshape(nx, units, width)
    out_ref[:, 2 * units :] = down_sum.reshape(nx, units, width)
    for copy in copies:
        copy.wait()


def outer_kernel(ask_ref, w_hbm_ref, out_ref, w_ref, rows_ref, sems):
    units = w_ref.shape[0] // 3
    width = w_ref.shape[1]
    n, step = rows_ref.shape[:2]
    pairs = [(w_hbm_ref, w_ref)] + [(ask_ref.at[i * step : (i + 1) * step], rows_ref.at[i]) for i in range(n)]
    copies = start_all(pairs, sems)
    copies.pop(0).wait()
    w_in, w_down = split(w_ref[: 2 * units]), split(w_ref[2 * units :])
    for i in range(n):
        copies[i].wait()
        in_sum, down_sum = weight_grad(w_in, w_down, [(rows_ref[i, :, :width], rows_ref[i, :, width:])])
        if i == 0:
            out_ref[: 2 * units] = in_sum
            out_ref[2 * units :] = down_sum
        else:
            out_ref[: 2 * units] += in_sum
            out_ref[2 * units :] += down_sum


def query_grad(rows, cots, w_gate, w_up, w_down, up_way, down_way):
    rows, cots = split(rows), split(cots)
    gate, up_part = dot3(rows, w_gate, up_way), dot3(rows, w_up, up_way)
    hidden_grad = dot3(cots, w_down, NT)
    _, active, slope = gates(gate)
    return dot3(split(hidden_grad * up_part * slope), w_gate, down_way) + dot3(
        split(hidden_grad * active), w_up, down_way
    )


def zero_kernel(q_ref, c_ref, wg_ref, wu_ref, wd_ref, out_ref):
    out_ref[...] = query_grad(
        q_ref[0], c_ref[0], split(wg_ref[0]), split(wu_ref[0]), split(wd_ref[0]), NN, NT
    )


def one_kernel(q_ref, c_ref, w_ref, zero_ref, out_ref):
    w_gate, w_up, w_down = [split(w) for w in parts(w_ref, w_ref.shape[1] // 3)]
    out_ref[0] = zero_ref[...]
    out_ref[1] = query_grad(q_ref[1], c_ref[1], w_gate, w_up, w_down, NT, NN)


def load_kernel(pair_ref, w_ref, pair_out_ref, w_out_ref, sems):
    for copy in start_all([(pair_ref, pair_out_ref), (w_ref, w_out_ref)], sems):
        copy.wait()


def final_kernel(d_ref, pair_ref, w_ref, new_ref, mine_ref, theirs_ref, new_out_ref, sems):
    copies = start_all([(new_ref, new_out_ref)], sems)
    width = d_ref.shape[2]
    units = d_ref.shape[1] // 3
    d_gate, d_up, d_down = [split(d) for d in parts(d_ref, units)]
    w_gate, w_up, w_down = [split(w) for w in parts(w_ref, units)]
    rows, cots = split(pair_ref[:, :width]), split(pair_ref[:, width:])
    gate, up_part = dot3(rows, w_gate, NT), dot3(rows, w_up, NT)
    hidden_grad = dot3(cots, w_down, NT)
    sigma, active, slope = gates(gate)
    bend = sigma * (1.0 - sigma) * (2.0 + gate * (1.0 - 2.0 * sigma))
    steep = slope * up_part
    d_g, d_u = dot3(rows, d_gate, NT), dot3(rows, d_up, NT)
    d_c = dot3(cots, d_down, NT)
    d_h = steep * d_g + active * d_u
    value = dot3(split(active * up_part), d_down, NN) + dot3(split(d_h), w_down, NN)
    to_gate = hidden_grad * (up_part * bend * d_g + slope * d_u) + steep * d_c
    to_up = hidden_grad * slope * d_g + active * d_c
    key = (
        dot3(split(hidden_grad * steep), d_gate, NN)
        + dot3(split(hidden_grad * active), d_up, NN)
        + dot3(split(to_gate), w_gate, NN)
        + dot3(split(to_up), w_up, NN)
    )
    tok = mine_ref.shape[0]
    mine_ref[:, :width] = key[:tok]
    mine_ref[:, width:] = value[:tok]
    theirs_ref[:, :width] = key[tok:]
    theirs_ref[:, width:] = value[tok:]
    copies[0].wait()


def join_kernel(scale, mine_ref, got_ref, rate_ref, k_ref, v_ref):
    width = k_ref.shape[1]
    k_ref[...] = scale * (mine_ref[:, :width] + got_ref[:, :width])
    rate = scale * rate_ref[...]
    for at in range(0, width, LANES):
        lanes = slice(width + at, width + at + LANES)
        v_ref[:, at : at + LANES] = rate * (mine_ref[:, lanes] + got_ref[:, lanes])


def after(value, *others):
    return lax.optimization_barrier((value, others))[0]


def both(*values):
    return lax.optimization_barrier(values)


def body(queries, keys, values, rates, grad_out, w_gate, w_up, w_down):
    tok, width = keys.shape
    hidden = w_gate.shape[2]
    n_z = lax.axis_size("z")
    units = hidden // (NX * NC)
    half = NX * units
    piece = 3 * units // n_z
    scale = float(tok * NX * NC * n_z) ** (-0.5)
    f32 = lambda *shape: jax.ShapeDtypeStruct(shape, jnp.float32)
    swap = lambda x: lax.ppermute(x, "c", [(i, (i + 1) % NC) for i in range(NC)])
    exchange = lambda x: lax.all_to_all(x.reshape(n_z, piece, width), "z", 0, 0)
    hold = lambda x: pltpu.with_memory_space_constraint(x, pltpu.HBM)
    n_mul = 2 * tok * width * half
    n_w = 12 * width * half
    here, there = pl.BlockSpec(memory_space=pltpu.VMEM), pl.BlockSpec(memory_space=pltpu.HBM)

    own, rate = call(
        pack_kernel,
        [f32(tok, 2 * width), f32(tok, LANES)],
        0,
        16 * tok * width,
        in_specs=[there] * 3,
        out_specs=[here] * 2,
        scratch_shapes=[
            pltpu.VMEM((tok, width), jnp.float32), pltpu.VMEM((1, tok), jnp.float32), pltpu.SemaphoreType.DMA((3,))
        ],
    )(hold(keys), hold(values), hold(rates.reshape(1, tok)))
    other = swap(own)
    w_rows = call(
        units_kernel,
        f32(NX, 3 * units, width),
        0,
        2 * n_w,
        in_specs=[there] * 3,
        out_specs=here,
        scratch_shapes=[pltpu.VMEM((2, width, half), jnp.float32), pltpu.SemaphoreType.DMA((2 + NX,))],
    )(hold(after(w_gate, own)), hold(w_up), hold(w_down))

    pair_shape = pltpu.HBM((2 * tok, 2 * width), jnp.float32)
    kept_shape = pltpu.HBM((NX, 3 * units, width), jnp.float32)
    inner, w_piece, ask, pair, kept = call(
        inner_kernel,
        [f32(NX, 3 * units, width), f32(piece, width), f32(tok, 2 * width), pair_shape, kept_shape],
        36 * n_mul,
        2 * n_w,
        in_specs=[here, here, here, there, there],
        out_specs=[here, here, here, there, there],
        scratch_shapes=[pltpu.SemaphoreType.DMA((5,))],
    )(own, other, w_rows, hold(queries), hold(grad_out))
    ask = lax.all_gather(ask, ("x", "c"), axis=0, tiled=True)
    inner = lax.all_to_all(inner, "x", 0, 0)
    inner = call(row_sum_kernel, f32(3 * units, width), 0, 2 * n_w)(inner)
    pieces = f32(n_z, piece, width)
    new = call(functools.partial(update_kernel, scale), pieces, 0, n_w)(exchange(inner), w_piece)
    new = exchange(new).reshape(3 * units, width)

    outer = call(
        outer_kernel,
        f32(3 * units, width),
        36 * n_mul,
        64 * tok * width,
        in_specs=[there, there],
        out_specs=here,
        scratch_shapes=[
            pltpu.VMEM((3 * units, width), jnp.float32),
            pltpu.VMEM((4, NX * NC * tok // 4, 2 * width), jnp.float32),
            pltpu.SemaphoreType.DMA((5,)),
        ],
    )(hold(ask), hold(new))
    new_all = lax.all_gather(new, ("x", "c"), axis=0, tiled=False)
    outer = call(total_kernel, pieces, 0, n_w)(exchange(outer))
    zero = call(zero_kernel, f32(tok, width), 30 * n_mul, 2 * n_w)(
        after(queries, outer), grad_out, w_gate, w_up, w_down
    )
    loaded = call(
        load_kernel,
        [f32(2 * tok, 2 * width), f32(NX, 3 * units, width)],
        0,
        4 * n_w,
        in_specs=[there] * 2,
        out_specs=[here] * 2,
        scratch_shapes=[pltpu.SemaphoreType.DMA((2,))],
    )(hold(after(pair, zero)), hold(kept))
    outer, loaded = both(exchange(outer).reshape(3 * units, width), loaded)
    d_all, new_all = both(lax.all_gather(outer, "x", axis=0, tiled=False), new_all)
    mine, theirs, new_all = call(
        final_kernel,
        [f32(tok, 2 * width)] * 2 + [f32(*new_all.shape)],
        72 * n_mul,
        3 * n_w,
        in_specs=[here, here, here, there],
        out_specs=[here] * 3,
        scratch_shapes=[pltpu.SemaphoreType.DMA((1,))],
    )(d_all, *loaded, hold(new_all))
    grad_queries = call(one_kernel, f32(2, tok, width), 30 * n_mul, 2 * n_w)(queries, grad_out, new_all, zero)
    theirs, grad_queries = both(swap(theirs), grad_queries)
    grad_keys, grad_values = call(
        functools.partial(join_kernel, scale), [f32(tok, width)] * 2, 0, 24 * tok * width
    )(mine, theirs, rate)
    return grad_queries, grad_keys, grad_values


def solution(mesh):
    devices = mesh.devices.reshape(-1, NX, NC, mesh.devices.shape[1])
    fine = Mesh(devices, ("z", "x", "c", "head"))
    ctx = ("z", "x", "c")
    in_specs = (
        P(None, ctx, "head"),
        P(ctx, "head"),
        P(ctx, "head"),
        P(ctx, "head"),
        P(None, ctx, "head"),
        P("head", None, None),
        P("head", None, None),
        P("head", None, None),
    )
    out_specs = (P(None, ctx, "head"), P(ctx, "head"), P(ctx, "head"))
    return jax.shard_map(body, mesh=fine, in_specs=in_specs, out_specs=out_specs, check_vma=False)
```

```python
import functools

import jax
import jax.numpy as jnp
from jax import lax
from jax.experimental import pallas as pl
from jax.experimental.pallas import tpu as pltpu
from jax.sharding import Mesh
from jax.sharding import PartitionSpec as P

NX, NC = 4, 2
NN = ((1,), (0,))
NT = ((1,), (1,))
MIB = 1 << 20
LANES = 128


def split(a):
    head = a.astype(jnp.bfloat16)
    tail = (a - head.astype(jnp.float32)).astype(jnp.bfloat16)
    return head, tail


def dot3(a, b, dims):
    rows = a[0].shape[0]
    dot = functools.partial(
        lax.dot_general, dimension_numbers=(dims, ((), ())), preferred_element_type=jnp.float32
    )
    both = dot(jnp.concatenate(a, axis=0), b[0])
    return both[:rows] + (both[rows:] + dot(a[0], b[1]))


def gates(gate):
    sigma = jax.nn.sigmoid(gate)
    return sigma, gate * sigma, sigma * (1.0 + gate * (1.0 - sigma))


def call(kernel, shapes, flops, n_bytes, limit=16, **more):
    return pl.pallas_call(
        kernel,
        out_shape=shapes,
        **more,
        compiler_params=pltpu.CompilerParams(vmem_limit_bytes=limit * MIB),
        cost_estimate=pl.CostEstimate(flops=flops, bytes_accessed=n_bytes, transcendentals=0),
    )


def start_all(pairs, sems):
    copies = [pltpu.make_async_copy(*pair, sems.at[i]) for i, pair in enumerate(pairs)]
    for copy in copies:
        copy.start()
    return copies


def pack_kernel(k_ref, v_ref, r_ref, inner_ref, rate_ref, raw_ref, row_ref, sems):
    width = k_ref.shape[1]
    tok = r_ref.shape[1]
    copies = start_all([(r_ref, row_ref), (v_ref, raw_ref), (k_ref, inner_ref.at[:, :width])], sems)
    copies[0].wait()
    rate = jnp.broadcast_to(row_ref[...], (LANES, tok)).T
    rate_ref[...] = rate
    copies[1].wait()
    for at in range(0, width, LANES):
        inner_ref[:, width + at : width + at + LANES] = rate * raw_ref[:, at : at + LANES]
    copies[2].wait()


def units_kernel(wg_ref, wu_ref, wd_ref, out_ref, raw_ref, sems):
    nx, rows, width = out_ref.shape
    units = rows // 3
    half = nx * units
    start = pl.multiple_of(lax.axis_index("c") * half, LANES)
    pairs = [
        (wg_ref.at[0, :, pl.ds(start, half)], raw_ref.at[0]),
        (wu_ref.at[0, :, pl.ds(start, half)], raw_ref.at[1]),
    ]
    pairs += [(wd_ref.at[0, pl.ds(start + i * units, units)], out_ref.at[i, 2 * units :]) for i in range(nx)]
    copies = start_all(pairs, sems)
    for i in range(2):
        copies[i].wait()
        out_ref[:, i * units : (i + 1) * units] = raw_ref[i].T.reshape(nx, units, width)
    for copy in copies[2:]:
        copy.wait()


def row_sum_kernel(in_ref, out_ref):
    total = in_ref[0]
    for i in range(1, in_ref.shape[0]):
        total += in_ref[i]
    out_ref[...] = total


def update_kernel(scale, in_ref, w_ref, out_ref):
    n = in_ref.shape[0]
    total = in_ref[0]
    for i in range(1, n):
        total += in_ref[i]
    total = w_ref[...] + scale * total
    for i in range(n):
        out_ref[i] = total


def total_kernel(in_ref, out_ref):
    n = in_ref.shape[0]
    total = in_ref[0]
    for i in range(1, n):
        total += in_ref[i]
    for i in range(n):
        out_ref[i] = total


def parts(ref, units):
    width = ref.shape[2]
    return [ref[:, i * units : (i + 1) * units].reshape(-1, width) for i in range(3)]


def weight_grad(w_in, w_down, chunks):
    n = w_down[0].shape[0]
    total = None
    for rows, cots in chunks:
        rows, cots = split(rows), split(cots)
        both = dot3(w_in, rows, NT)
        hidden_grad = dot3(w_down, cots, NT)
        up_part = both[n:]
        _, active, slope = gates(both[:n])
        in_grad = jnp.concatenate([hidden_grad * up_part * slope, hidden_grad * active], axis=0)
        new = dot3(split(in_grad), rows, NN), dot3(split(active * up_part), cots, NN)
        total = new if total is None else (total[0] + new[0], total[1] + new[1])
    return total


def inner_kernel(own_ref, other_ref, w_ref, q_ref, c_ref, out_ref, piece_ref, ask_ref, pair_ref, kept_ref, sems):
    nx, rows, width = w_ref.shape
    units = rows // 3
    n = nx * units
    tok = own_ref.shape[0]
    pairs = [(q_ref.at[1], ask_ref.at[:, :width]), (c_ref.at[1], ask_ref.at[:, width:])]
    pairs += [(own_ref, pair_ref.at[:tok]), (other_ref, pair_ref.at[tok:]), (w_ref, kept_ref)]
    copies = start_all(pairs, sems)
    piece = piece_ref.shape[0]
    start = pl.multiple_of(lax.axis_index("z") * piece, 8)
    piece_ref[...] = w_ref[lax.axis_index("x"), pl.ds(start, piece)]
    w_gate, w_up, w_down = parts(w_ref, units)
    pair = jnp.concatenate([own_ref[...], other_ref[...]], axis=0)
    in_sum, down_sum = weight_grad(
        split(jnp.concatenate([w_gate, w_up], axis=0)), split(w_down), [(pair[:, :width], pair[:, width:])]
    )
    out_ref[:, :units] = in_sum[:n].reshape(nx, units, width)
    out_ref[:, units : 2 * units] = in_sum[n:].reshape(nx, units, width)
    out_ref[:, 2 * units :] = down_sum.reshape(nx, units, width)
    for copy in copies:
        copy.wait()


def outer_kernel(rows_ref, w_ref, out_ref, new_ref, sems):
    copies = start_all([(w_ref, new_ref)], sems)
    width = w_ref.shape[1]
    units = w_ref.shape[0] // 3
    step = 256
    chunks = [
        (rows_ref[at : at + step, :width], rows_ref[at : at + step, width:])
        for at in range(0, rows_ref.shape[0], step)
    ]
    in_sum, down_sum = weight_grad(split(w_ref[: 2 * units]), split(w_ref[2 * units :]), chunks)
    out_ref[: 2 * units] = in_sum
    out_ref[2 * units :] = down_sum
    copies[0].wait()


def query_grad(rows, cots, w_gate, w_up, w_down, up_way, down_way):
    rows, cots = split(rows), split(cots)
    gate, up_part = dot3(rows, w_gate, up_way), dot3(rows, w_up, up_way)
    hidden_grad = dot3(cots, w_down, NT)
    _, active, slope = gates(gate)
    return dot3(split(hidden_grad * up_part * slope), w_gate, down_way) + dot3(
        split(hidden_grad * active), w_up, down_way
    )


def zero_kernel(q_hbm_ref, c_hbm_ref, wg_hbm_ref, wu_hbm_ref, wd_hbm_ref, out_ref, *refs):
    *refs, sems = refs
    pairs = [(ref.at[0], to) for ref, to in zip((q_hbm_ref, c_hbm_ref, wg_hbm_ref, wu_hbm_ref, wd_hbm_ref), refs)]
    for copy in start_all(pairs, sems):
        copy.wait()
    q_ref, c_ref, wg_ref, wu_ref, wd_ref = refs
    out_ref[...] = query_grad(
        q_ref[...], c_ref[...], split(wg_ref[...]), split(wu_ref[...]), split(wd_ref[...]), NN, NT
    )


def one_kernel(q_ref, c_ref, w_ref, zero_ref, out_ref):
    w_gate, w_up, w_down = [split(w) for w in parts(w_ref, w_ref.shape[1] // 3)]
    out_ref[0] = zero_ref[...]
    out_ref[1] = query_grad(q_ref[...], c_ref[...], w_gate, w_up, w_down, NT, NN)


def load_kernel(*refs):
    *refs, sems = refs
    n = len(refs) // 2
    for copy in start_all(list(zip(refs[:n], refs[n:])), sems):
        copy.wait()


def final_kernel(
    d_ref, pair_ref, w_ref, new_ref, q_ref, c_ref, mine_ref, theirs_ref, new_out_ref, q_out_ref, c_out_ref, sems
):
    copies = start_all([(new_ref, new_out_ref), (q_ref.at[1], q_out_ref), (c_ref.at[1], c_out_ref)], sems)
    width = d_ref.shape[2]
    units = d_ref.shape[1] // 3
    d_gate, d_up, d_down = [split(d) for d in parts(d_ref, units)]
    w_gate, w_up, w_down = [split(w) for w in parts(w_ref, units)]
    rows, cots = split(pair_ref[:, :width]), split(pair_ref[:, width:])
    gate, up_part = dot3(rows, w_gate, NT), dot3(rows, w_up, NT)
    hidden_grad = dot3(cots, w_down, NT)
    sigma, active, slope = gates(gate)
    bend = sigma * (1.0 - sigma) * (2.0 + gate * (1.0 - 2.0 * sigma))
    steep = slope * up_part
    d_g, d_u = dot3(rows, d_gate, NT), dot3(rows, d_up, NT)
    d_c = dot3(cots, d_down, NT)
    d_h = steep * d_g + active * d_u
    value = dot3(split(active * up_part), d_down, NN) + dot3(split(d_h), w_down, NN)
    to_gate = hidden_grad * (up_part * bend * d_g + slope * d_u) + steep * d_c
    to_up = hidden_grad * slope * d_g + active * d_c
    key = (
        dot3(split(hidden_grad * steep), d_gate, NN)
        + dot3(split(hidden_grad * active), d_up, NN)
        + dot3(split(to_gate), w_gate, NN)
        + dot3(split(to_up), w_up, NN)
    )
    tok = mine_ref.shape[0]
    mine_ref[:, :width] = key[:tok]
    mine_ref[:, width:] = value[:tok]
    theirs_ref[:, :width] = key[tok:]
    theirs_ref[:, width:] = value[tok:]
    for copy in copies:
        copy.wait()


def join_kernel(scale, mine_ref, got_ref, rate_ref, k_ref, v_ref):
    width = k_ref.shape[1]
    k_ref[...] = scale * (mine_ref[:, :width] + got_ref[:, :width])
    rate = scale * rate_ref[...]
    for at in range(0, width, LANES):
        lanes = slice(width + at, width + at + LANES)
        v_ref[:, at : at + LANES] = rate * (mine_ref[:, lanes] + got_ref[:, lanes])


def after(value, *others):
    return lax.optimization_barrier((value, others))[0]


def both(*values):
    return lax.optimization_barrier(values)


def body(queries, keys, values, rates, grad_out, w_gate, w_up, w_down):
    tok, width = keys.shape
    hidden = w_gate.shape[2]
    n_z = lax.axis_size("z")
    units = hidden // (NX * NC)
    half = NX * units
    piece = 3 * units // n_z
    scale = float(tok * NX * NC * n_z) ** (-0.5)
    f32 = lambda *shape: jax.ShapeDtypeStruct(shape, jnp.float32)
    swap = lambda x: lax.ppermute(x, "c", [(i, (i + 1) % NC) for i in range(NC)])
    exchange = lambda x: lax.all_to_all(x.reshape(n_z, piece, width), "z", 0, 0)
    hold = lambda x: pltpu.with_memory_space_constraint(x, pltpu.HBM)
    n_mul = 2 * tok * width * half
    n_w = 12 * width * half
    here, there = pl.BlockSpec(memory_space=pltpu.VMEM), pl.BlockSpec(memory_space=pltpu.HBM)

    own, rate = call(
        pack_kernel,
        [f32(tok, 2 * width), f32(tok, LANES)],
        0,
        16 * tok * width,
        in_specs=[there] * 3,
        out_specs=[here] * 2,
        scratch_shapes=[
            pltpu.VMEM((tok, width), jnp.float32), pltpu.VMEM((1, tok), jnp.float32), pltpu.SemaphoreType.DMA((3,))
        ],
    )(hold(keys), hold(values), hold(rates.reshape(1, tok)))
    other = swap(own)
    w_rows = call(
        units_kernel,
        f32(NX, 3 * units, width),
        0,
        2 * n_w,
        in_specs=[there] * 3,
        out_specs=here,
        scratch_shapes=[pltpu.VMEM((2, width, half), jnp.float32), pltpu.SemaphoreType.DMA((2 + NX,))],
    )(hold(after(w_gate, own)), hold(w_up), hold(w_down))

    pair_shape = pltpu.HBM((2 * tok, 2 * width), jnp.float32)
    kept_shape = pltpu.HBM((NX, 3 * units, width), jnp.float32)
    inner, w_piece, ask, pair, kept = call(
        inner_kernel,
        [f32(NX, 3 * units, width), f32(piece, width), f32(tok, 2 * width), pair_shape, kept_shape],
        36 * n_mul,
        2 * n_w,
        in_specs=[here, here, here, there, there],
        out_specs=[here, here, here, there, there],
        scratch_shapes=[pltpu.SemaphoreType.DMA((5,))],
    )(own, other, w_rows, hold(queries), hold(grad_out))
    ask = lax.all_gather(ask, ("x", "c"), axis=0, tiled=True)
    inner = lax.all_to_all(inner, "x", 0, 0)
    inner = call(row_sum_kernel, f32(3 * units, width), 0, 2 * n_w)(inner)
    pieces = f32(n_z, piece, width)
    new = call(functools.partial(update_kernel, scale), pieces, 0, n_w)(exchange(inner), w_piece)
    load = lambda *args: call(
        load_kernel,
        [f32(*a.shape) for a in args],
        0,
        8 * sum(a.size for a in args),
        in_specs=[there] * len(args),
        out_specs=[here] * len(args),
        scratch_shapes=[pltpu.SemaphoreType.DMA((len(args),))],
    )(*[hold(a) for a in args])
    (ask,) = load(after(ask, new))
    new, ask = both(exchange(new).reshape(3 * units, width), ask)

    outer, new = call(
        outer_kernel,
        [f32(3 * units, width), pltpu.HBM((3 * units, width), jnp.float32)],
        36 * n_mul,
        64 * tok * width,
        in_specs=[here, here],
        out_specs=[here, there],
        scratch_shapes=[pltpu.SemaphoreType.DMA((1,))],
    )(ask, new)
    new_all = lax.all_gather(new, ("x", "c"), axis=0, tiled=False)
    outer = call(total_kernel, pieces, 0, n_w)(exchange(outer))
    vmem = lambda *shape: pltpu.VMEM(shape, jnp.float32)
    zero = call(
        zero_kernel,
        f32(tok, width),
        30 * n_mul,
        2 * n_w,
        in_specs=[there] * 5,
        out_specs=here,
        scratch_shapes=[
            vmem(tok, width), vmem(tok, width), vmem(width, hidden), vmem(width, hidden), vmem(hidden, width),
            pltpu.SemaphoreType.DMA((5,)),
        ],
    )(*[hold(a) for a in (after(queries, outer), grad_out, w_gate, w_up, w_down)])
    loaded = load(after(pair, zero), kept)
    outer, loaded = both(exchange(outer).reshape(3 * units, width), loaded)
    d_all, new_all = both(lax.all_gather(outer, "x", axis=0, tiled=False), new_all)
    mine, theirs, *ones = call(
        final_kernel,
        [f32(tok, 2 * width)] * 2 + [f32(*new_all.shape), f32(tok, width), f32(tok, width)],
        72 * n_mul,
        3 * n_w,
        in_specs=[here, here, here, there, there, there],
        out_specs=[here] * 5,
        scratch_shapes=[pltpu.SemaphoreType.DMA((3,))],
    )(d_all, *loaded, *[hold(a) for a in (new_all, queries, grad_out)])
    new_all, q_one, c_one = ones
    grad_queries = call(one_kernel, f32(2, tok, width), 30 * n_mul, 2 * n_w)(q_one, c_one, new_all, zero)
    theirs, grad_queries = both(swap(theirs), grad_queries)
    grad_keys, grad_values = call(
        functools.partial(join_kernel, scale), [f32(tok, width)] * 2, 0, 24 * tok * width
    )(mine, theirs, rate)
    return grad_queries, grad_keys, grad_values


def solution(mesh):
    devices = mesh.devices.reshape(-1, NX, NC, mesh.devices.shape[1])
    fine = Mesh(devices, ("z", "x", "c", "head"))
    ctx = ("z", "x", "c")
    in_specs = (
        P(None, ctx, "head"),
        P(ctx, "head"),
        P(ctx, "head"),
        P(ctx, "head"),
        P(None, ctx, "head"),
        P("head", None, None),
        P("head", None, None),
        P("head", None, None),
    )
    out_specs = (P(None, ctx, "head"), P(ctx, "head"), P(ctx, "head"))
    return jax.shard_map(body, mesh=fine, in_specs=in_specs, out_specs=out_specs, check_vma=False)
```

```python
import functools

import jax
import jax.numpy as jnp
from jax import lax
from jax.experimental import pallas as pl
from jax.experimental.pallas import tpu as pltpu
from jax.sharding import Mesh
from jax.sharding import PartitionSpec as P

NX, NC = 4, 2
NN = ((1,), (0,))
NT = ((1,), (1,))
MIB = 1 << 20
LANES = 128


def split(a):
    head = a.astype(jnp.bfloat16)
    tail = (a - head.astype(jnp.float32)).astype(jnp.bfloat16)
    return head, tail


def dot3(a, b, dims):
    rows = a[0].shape[0]
    dot = functools.partial(
        lax.dot_general, dimension_numbers=(dims, ((), ())), preferred_element_type=jnp.float32
    )
    both = dot(jnp.concatenate(a, axis=0), b[0])
    return both[:rows] + (both[rows:] + dot(a[0], b[1]))


def gates(gate):
    sigma = jax.nn.sigmoid(gate)
    return sigma, gate * sigma, sigma * (1.0 + gate * (1.0 - sigma))


def call(kernel, shapes, flops, n_bytes, limit=16, **more):
    return pl.pallas_call(
        kernel,
        out_shape=shapes,
        **more,
        compiler_params=pltpu.CompilerParams(vmem_limit_bytes=limit * MIB),
        cost_estimate=pl.CostEstimate(flops=flops, bytes_accessed=n_bytes, transcendentals=0),
    )


def start_all(pairs, sems):
    copies = [pltpu.make_async_copy(*pair, sems.at[i]) for i, pair in enumerate(pairs)]
    for copy in copies:
        copy.start()
    return copies


def pack_kernel(k_ref, v_ref, r_ref, inner_ref, rate_ref, raw_ref, row_ref, sems):
    width = k_ref.shape[1]
    tok = r_ref.shape[1]
    copies = start_all([(r_ref, row_ref), (v_ref, raw_ref), (k_ref, inner_ref.at[:, :width])], sems)
    copies[0].wait()
    rate = jnp.broadcast_to(row_ref[...], (LANES, tok)).T
    rate_ref[...] = rate
    copies[1].wait()
    for at in range(0, width, LANES):
        inner_ref[:, width + at : width + at + LANES] = rate * raw_ref[:, at : at + LANES]
    copies[2].wait()


def units_kernel(wg_ref, wu_ref, wd_ref, q_ref, c_ref, out_ref, ask_ref, raw_ref, sems):
    nx, rows, width = out_ref.shape
    units = rows // 3
    half = nx * units
    start = pl.multiple_of(lax.axis_index("c") * half, LANES)
    pairs = [
        (wg_ref.at[0, :, pl.ds(start, half)], raw_ref.at[0]),
        (wu_ref.at[0, :, pl.ds(start, half)], raw_ref.at[1]),
    ]
    pairs += [(wd_ref.at[0, pl.ds(start + i * units, units)], out_ref.at[i, 2 * units :]) for i in range(nx)]
    pairs += [(q_ref.at[1], ask_ref.at[:, :width]), (c_ref.at[1], ask_ref.at[:, width:])]
    copies = start_all(pairs, sems)
    for i in range(2):
        copies[i].wait()
        out_ref[:, i * units : (i + 1) * units] = raw_ref[i].T.reshape(nx, units, width)
    for copy in copies[2:]:
        copy.wait()


def row_sum_kernel(in_ref, out_ref):
    total = in_ref[0]
    for i in range(1, in_ref.shape[0]):
        total += in_ref[i]
    out_ref[...] = total


def update_kernel(scale, in_ref, w_ref, out_ref):
    n = in_ref.shape[0]
    total = in_ref[0]
    for i in range(1, n):
        total += in_ref[i]
    total = w_ref[...] + scale * total
    for i in range(n):
        out_ref[i] = total


def total_kernel(in_ref, out_ref):
    n = in_ref.shape[0]
    total = in_ref[0]
    for i in range(1, n):
        total += in_ref[i]
    for i in range(n):
        out_ref[i] = total


def parts(ref, units):
    width = ref.shape[2]
    return [ref[:, i * units : (i + 1) * units].reshape(-1, width) for i in range(3)]


def weight_grad(w_in, w_down, chunks):
    n = w_down[0].shape[0]
    total = None
    for rows, cots in chunks:
        rows, cots = split(rows), split(cots)
        both = dot3(w_in, rows, NT)
        hidden_grad = dot3(w_down, cots, NT)
        up_part = both[n:]
        _, active, slope = gates(both[:n])
        in_grad = jnp.concatenate([hidden_grad * up_part * slope, hidden_grad * active], axis=0)
        new = dot3(split(in_grad), rows, NN), dot3(split(active * up_part), cots, NN)
        total = new if total is None else (total[0] + new[0], total[1] + new[1])
    return total


def inner_kernel(own_ref, other_ref, w_ref, asked_ref, out_ref, piece_ref, ask_ref, pair_ref, kept_ref, sems):
    nx, rows, width = w_ref.shape
    units = rows // 3
    n = nx * units
    tok = own_ref.shape[0]
    pairs = [(asked_ref, ask_ref), (own_ref, pair_ref.at[:tok]), (other_ref, pair_ref.at[tok:]), (w_ref, kept_ref)]
    copies = start_all(pairs, sems)
    piece = piece_ref.shape[0]
    start = pl.multiple_of(lax.axis_index("z") * piece, 8)
    piece_ref[...] = w_ref[lax.axis_index("x"), pl.ds(start, piece)]
    w_gate, w_up, w_down = parts(w_ref, units)
    pair = jnp.concatenate([own_ref[...], other_ref[...]], axis=0)
    in_sum, down_sum = weight_grad(
        split(jnp.concatenate([w_gate, w_up], axis=0)), split(w_down), [(pair[:, :width], pair[:, width:])]
    )
    out_ref[:, :units] = in_sum[:n].reshape(nx, units, width)
    out_ref[:, units : 2 * units] = in_sum[n:].reshape(nx, units, width)
    out_ref[:, 2 * units :] = down_sum.reshape(nx, units, width)
    for copy in copies:
        copy.wait()


def outer_kernel(ask_ref, w_ref, out_ref, new_ref, rows_ref, sems):
    width = w_ref.shape[1]
    units = w_ref.shape[0] // 3
    tokens = ask_ref.shape[0]
    cuts = [0, 128, *range(256, tokens + 1, 256)]
    spans = [slice(*pair) for pair in zip(cuts, cuts[1:])]
    pairs = [(ask_ref.at[span], rows_ref.at[span]) for span in spans]
    *copies, last = start_all(pairs + [(w_ref, new_ref)], sems)
    w_in, w_down = split(w_ref[: 2 * units]), split(w_ref[2 * units :])
    for span, copy in zip(spans, copies):
        copy.wait()
        in_sum, down_sum = weight_grad(w_in, w_down, [(rows_ref[span, :width], rows_ref[span, width:])])
        if span.start == 0:
            out_ref[: 2 * units] = in_sum
            out_ref[2 * units :] = down_sum
        else:
            out_ref[: 2 * units] += in_sum
            out_ref[2 * units :] += down_sum
    last.wait()


def query_grad(rows, cots, w_gate, w_up, w_down, up_way, down_way):
    rows, cots = split(rows), split(cots)
    gate, up_part = dot3(rows, w_gate, up_way), dot3(rows, w_up, up_way)
    hidden_grad = dot3(cots, w_down, NT)
    _, active, slope = gates(gate)
    return dot3(split(hidden_grad * up_part * slope), w_gate, down_way) + dot3(
        split(hidden_grad * active), w_up, down_way
    )


def zero_kernel(q_hbm_ref, c_hbm_ref, wg_hbm_ref, wu_hbm_ref, wd_hbm_ref, out_ref, *refs):
    *refs, sems = refs
    pairs = [(ref.at[0], to) for ref, to in zip((q_hbm_ref, c_hbm_ref, wg_hbm_ref, wu_hbm_ref, wd_hbm_ref), refs)]
    for copy in start_all(pairs, sems):
        copy.wait()
    q_ref, c_ref, wg_ref, wu_ref, wd_ref = refs
    out_ref[...] = query_grad(
        q_ref[...], c_ref[...], split(wg_ref[...]), split(wu_ref[...]), split(wd_ref[...]), NN, NT
    )


def one_kernel(q_ref, c_ref, w_ref, zero_ref, out_ref):
    w_gate, w_up, w_down = [split(w) for w in parts(w_ref, w_ref.shape[1] // 3)]
    out_ref[0] = zero_ref[...]
    out_ref[1] = query_grad(q_ref[...], c_ref[...], w_gate, w_up, w_down, NT, NN)


def prepare_kernel(
    pair_hbm_ref, w_hbm_ref, pair_ref, w_ref, gate_ref, up_ref, grad_ref, sems
):
    for copy in start_all([(pair_hbm_ref, pair_ref), (w_hbm_ref, w_ref)], sems):
        copy.wait()
    width = w_ref.shape[2]
    w_gate, w_up, w_down = [split(w) for w in parts(w_ref, w_ref.shape[1] // 3)]
    rows, cots = split(pair_ref[:, :width]), split(pair_ref[:, width:])
    gate_ref[...] = dot3(rows, w_gate, NT)
    up_ref[...] = dot3(rows, w_up, NT)
    grad_ref[...] = dot3(cots, w_down, NT)


def final_kernel(
    d_ref, pair_ref, w_ref, gate_ref, up_ref, grad_ref, new_ref, q_ref, c_ref, mine_ref, theirs_ref, new_out_ref, q_out_ref, c_out_ref, sems
):
    copies = start_all([(new_ref, new_out_ref), (q_ref.at[1], q_out_ref), (c_ref.at[1], c_out_ref)], sems)
    width = d_ref.shape[2]
    units = d_ref.shape[1] // 3
    d_gate, d_up, d_down = [split(d) for d in parts(d_ref, units)]
    w_gate, w_up, w_down = [split(w) for w in parts(w_ref, units)]
    rows, cots = split(pair_ref[:, :width]), split(pair_ref[:, width:])
    gate, up_part, hidden_grad = gate_ref[...], up_ref[...], grad_ref[...]
    sigma, active, slope = gates(gate)
    bend = sigma * (1.0 - sigma) * (2.0 + gate * (1.0 - 2.0 * sigma))
    steep = slope * up_part
    d_g, d_u = dot3(rows, d_gate, NT), dot3(rows, d_up, NT)
    d_c = dot3(cots, d_down, NT)
    d_h = steep * d_g + active * d_u
    value = dot3(split(active * up_part), d_down, NN) + dot3(split(d_h), w_down, NN)
    to_gate = hidden_grad * (up_part * bend * d_g + slope * d_u) + steep * d_c
    to_up = hidden_grad * slope * d_g + active * d_c
    key = (
        dot3(split(hidden_grad * steep), d_gate, NN)
        + dot3(split(hidden_grad * active), d_up, NN)
        + dot3(split(to_gate), w_gate, NN)
        + dot3(split(to_up), w_up, NN)
    )
    tok = mine_ref.shape[0]
    mine_ref[:, :width] = key[:tok]
    mine_ref[:, width:] = value[:tok]
    theirs_ref[:, :width] = key[tok:]
    theirs_ref[:, width:] = value[tok:]
    for copy in copies:
        copy.wait()


def join_kernel(scale, mine_ref, got_ref, rate_ref, k_ref, v_ref):
    width = k_ref.shape[1]
    k_ref[...] = scale * (mine_ref[:, :width] + got_ref[:, :width])
    rate = scale * rate_ref[...]
    for at in range(0, width, LANES):
        lanes = slice(width + at, width + at + LANES)
        v_ref[:, at : at + LANES] = rate * (mine_ref[:, lanes] + got_ref[:, lanes])


def after(value, *others):
    return lax.optimization_barrier((value, others))[0]


def both(*values):
    return lax.optimization_barrier(values)


def body(queries, keys, values, rates, grad_out, w_gate, w_up, w_down):
    tok, width = keys.shape
    hidden = w_gate.shape[2]
    n_z = lax.axis_size("z")
    units = hidden // (NX * NC)
    half = NX * units
    piece = 3 * units // n_z
    scale = float(tok * NX * NC * n_z) ** (-0.5)
    f32 = lambda *shape: jax.ShapeDtypeStruct(shape, jnp.float32)
    swap = lambda x: lax.ppermute(x, "c", [(i, (i + 1) % NC) for i in range(NC)])
    exchange = lambda x: lax.all_to_all(x.reshape(n_z, piece, width), "z", 0, 0)
    hold = lambda x: pltpu.with_memory_space_constraint(x, pltpu.HBM)
    n_mul = 2 * tok * width * half
    n_w = 12 * width * half
    here, there = pl.BlockSpec(memory_space=pltpu.VMEM), pl.BlockSpec(memory_space=pltpu.HBM)

    own, rate = call(
        pack_kernel,
        [f32(tok, 2 * width), f32(tok, LANES)],
        0,
        16 * tok * width,
        in_specs=[there] * 3,
        out_specs=[here] * 2,
        scratch_shapes=[
            pltpu.VMEM((tok, width), jnp.float32), pltpu.VMEM((1, tok), jnp.float32), pltpu.SemaphoreType.DMA((3,))
        ],
    )(hold(keys), hold(values), hold(rates.reshape(1, tok)))
    other = swap(own)
    w_rows, ask = call(
        units_kernel,
        [f32(NX, 3 * units, width), f32(tok, 2 * width)],
        0,
        2 * n_w,
        in_specs=[there] * 5,
        out_specs=[here] * 2,
        scratch_shapes=[pltpu.VMEM((2, width, half), jnp.float32), pltpu.SemaphoreType.DMA((4 + NX,))],
    )(*[hold(a) for a in (after(w_gate, own), w_up, w_down, queries, grad_out)])

    pair_shape = pltpu.HBM((2 * tok, 2 * width), jnp.float32)
    ask_shape = pltpu.HBM((tok, 2 * width), jnp.float32)
    kept_shape = pltpu.HBM((NX, 3 * units, width), jnp.float32)
    inner, w_piece, ask, pair, kept = call(
        inner_kernel,
        [f32(NX, 3 * units, width), f32(piece, width), ask_shape, pair_shape, kept_shape],
        36 * n_mul,
        2 * n_w,
        in_specs=[here] * 4,
        out_specs=[here, here, there, there, there],
        scratch_shapes=[pltpu.SemaphoreType.DMA((4,))],
    )(own, other, w_rows, ask)
    ask = lax.all_gather(ask, ("x", "c"), axis=0, tiled=True)
    inner = lax.all_to_all(inner, "x", 0, 0)
    inner = call(row_sum_kernel, f32(3 * units, width), 0, 2 * n_w)(inner)
    pieces = f32(n_z, piece, width)
    new = call(functools.partial(update_kernel, scale), pieces, 0, n_w)(exchange(inner), w_piece)
    new = exchange(new).reshape(3 * units, width)

    outer, new = call(
        outer_kernel,
        [f32(3 * units, width), pltpu.HBM((3 * units, width), jnp.float32)],
        36 * n_mul,
        64 * tok * width,
        in_specs=[there, here],
        out_specs=[here, there],
        scratch_shapes=[pltpu.VMEM(ask.shape, jnp.float32), pltpu.SemaphoreType.DMA((6,))],
    )(hold(ask), new)
    new_all = lax.all_gather(new, ("x", "c"), axis=0, tiled=False)
    outer = call(total_kernel, pieces, 0, n_w)(exchange(outer))
    vmem = lambda *shape: pltpu.VMEM(shape, jnp.float32)
    zero = call(
        zero_kernel,
        f32(tok, width),
        30 * n_mul,
        2 * n_w,
        in_specs=[there] * 5,
        out_specs=here,
        scratch_shapes=[
            vmem(tok, width), vmem(tok, width), vmem(width, hidden), vmem(width, hidden), vmem(hidden, width),
            pltpu.SemaphoreType.DMA((5,)),
        ],
    )(*[hold(a) for a in (after(queries, outer), grad_out, w_gate, w_up, w_down)])
    loaded = call(
        prepare_kernel,
        [f32(2 * tok, 2 * width), f32(NX, 3 * units, width)] + [f32(2 * tok, half)] * 3,
        18 * n_mul,
        4 * n_w,
        in_specs=[there] * 2,
        out_specs=[here] * 5,
        scratch_shapes=[pltpu.SemaphoreType.DMA((2,))],
    )(hold(after(pair, zero)), hold(kept))
    outer, loaded = both(exchange(outer).reshape(3 * units, width), loaded)
    d_all, new_all = both(lax.all_gather(outer, "x", axis=0, tiled=False), new_all)
    mine, theirs, *ones = call(
        final_kernel,
        [f32(tok, 2 * width)] * 2 + [f32(*new_all.shape), f32(tok, width), f32(tok, width)],
        72 * n_mul,
        3 * n_w,
        in_specs=[here] * 6 + [there] * 3,
        out_specs=[here] * 5,
        scratch_shapes=[pltpu.SemaphoreType.DMA((3,))],
    )(d_all, *loaded, *[hold(a) for a in (new_all, queries, grad_out)])
    new_all, q_one, c_one = ones
    grad_queries = call(one_kernel, f32(2, tok, width), 30 * n_mul, 2 * n_w)(q_one, c_one, new_all, zero)
    theirs, grad_queries = both(swap(theirs), grad_queries)
    grad_keys, grad_values = call(
        functools.partial(join_kernel, scale), [f32(tok, width)] * 2, 0, 24 * tok * width
    )(mine, theirs, rate)
    return grad_queries, grad_keys, grad_values


def solution(mesh):
    devices = mesh.devices.reshape(-1, NX, NC, mesh.devices.shape[1])
    fine = Mesh(devices, ("z", "x", "c", "head"))
    ctx = ("z", "x", "c")
    in_specs = (
        P(None, ctx, "head"),
        P(ctx, "head"),
        P(ctx, "head"),
        P(ctx, "head"),
        P(None, ctx, "head"),
        P("head", None, None),
        P("head", None, None),
        P("head", None, None),
    )
    out_specs = (P(None, ctx, "head"), P(ctx, "head"), P(ctx, "head"))
    return jax.shard_map(body, mesh=fine, in_specs=in_specs, out_specs=out_specs, check_vma=False)
```

```python
import functools

import jax
import jax.numpy as jnp
from jax import lax
from jax.experimental import pallas as pl
from jax.experimental.pallas import tpu as pltpu
from jax.sharding import Mesh
from jax.sharding import PartitionSpec as P

NX, NC = 4, 2
NN = ((1,), (0,))
NT = ((1,), (1,))
MIB = 1 << 20
LANES = 128


def split(a):
    head = a.astype(jnp.bfloat16)
    tail = (a - head.astype(jnp.float32)).astype(jnp.bfloat16)
    return head, tail


def dot3(a, b, dims):
    rows = a[0].shape[0]
    dot = functools.partial(
        lax.dot_general, dimension_numbers=(dims, ((), ())), preferred_element_type=jnp.float32
    )
    both = dot(jnp.concatenate(a, axis=0), b[0])
    return both[:rows] + (both[rows:] + dot(a[0], b[1]))


def gates(gate):
    sigma = jax.nn.sigmoid(gate)
    return sigma, gate * sigma, sigma * (1.0 + gate * (1.0 - sigma))


def call(kernel, shapes, flops, n_bytes, limit=16, **more):
    return pl.pallas_call(
        kernel,
        out_shape=shapes,
        **more,
        compiler_params=pltpu.CompilerParams(vmem_limit_bytes=limit * MIB),
        cost_estimate=pl.CostEstimate(flops=flops, bytes_accessed=n_bytes, transcendentals=0),
    )


def start_all(pairs, sems):
    copies = [pltpu.make_async_copy(*pair, sems.at[i]) for i, pair in enumerate(pairs)]
    for copy in copies:
        copy.start()
    return copies


def pack_kernel(k_ref, v_ref, r_ref, inner_ref, rate_ref, raw_ref, row_ref, sems):
    width = k_ref.shape[1]
    tok = r_ref.shape[1]
    copies = start_all([(r_ref, row_ref), (v_ref, raw_ref), (k_ref, inner_ref.at[:, :width])], sems)
    copies[0].wait()
    rate = jnp.broadcast_to(row_ref[...], (LANES, tok)).T
    rate_ref[...] = rate
    copies[1].wait()
    for at in range(0, width, LANES):
        inner_ref[:, width + at : width + at + LANES] = rate * raw_ref[:, at : at + LANES]
    copies[2].wait()


def units_kernel(wg_ref, wu_ref, wd_ref, q_ref, c_ref, out_ref, ask_ref, raw_ref, sems):
    nx, rows, width = out_ref.shape
    units = rows // 3
    half = nx * units
    start = pl.multiple_of(lax.axis_index("c") * half, LANES)
    pairs = [
        (wg_ref.at[0, :, pl.ds(start, half)], raw_ref.at[0]),
        (wu_ref.at[0, :, pl.ds(start, half)], raw_ref.at[1]),
    ]
    pairs += [(wd_ref.at[0, pl.ds(start + i * units, units)], out_ref.at[i, 2 * units :]) for i in range(nx)]
    pairs += [(q_ref.at[1], ask_ref.at[:, :width]), (c_ref.at[1], ask_ref.at[:, width:])]
    copies = start_all(pairs, sems)
    for i in range(2):
        copies[i].wait()
        out_ref[:, i * units : (i + 1) * units] = raw_ref[i].T.reshape(nx, units, width)
    for copy in copies[2:]:
        copy.wait()


def row_sum_kernel(in_ref, out_ref):
    total = in_ref[0]
    for i in range(1, in_ref.shape[0]):
        total += in_ref[i]
    out_ref[...] = total


def update_kernel(scale, in_ref, w_ref, out_ref):
    n = in_ref.shape[0]
    total = in_ref[0]
    for i in range(1, n):
        total += in_ref[i]
    total = w_ref[...] + scale * total
    for i in range(n):
        out_ref[i] = total


def total_kernel(in_ref, out_ref):
    n = in_ref.shape[0]
    total = in_ref[0]
    for i in range(1, n):
        total += in_ref[i]
    for i in range(n):
        out_ref[i] = total


def parts(ref, units):
    width = ref.shape[2]
    return [ref[:, i * units : (i + 1) * units].reshape(-1, width) for i in range(3)]


def weight_grad(w_in, w_down, chunks):
    n = w_down[0].shape[0]
    total = None
    for rows, cots in chunks:
        rows, cots = split(rows), split(cots)
        both = dot3(w_in, rows, NT)
        hidden_grad = dot3(w_down, cots, NT)
        up_part = both[n:]
        _, active, slope = gates(both[:n])
        in_grad = jnp.concatenate([hidden_grad * up_part * slope, hidden_grad * active], axis=0)
        new = dot3(split(in_grad), rows, NN), dot3(split(active * up_part), cots, NN)
        total = new if total is None else (total[0] + new[0], total[1] + new[1])
    return total


def inner_kernel(own_ref, other_ref, w_ref, asked_ref, out_ref, piece_ref, ask_ref, pair_ref, kept_ref, sems):
    nx, rows, width = w_ref.shape
    units = rows // 3
    n = nx * units
    tok = own_ref.shape[0]
    pairs = [(asked_ref, ask_ref), (own_ref, pair_ref.at[:tok]), (other_ref, pair_ref.at[tok:]), (w_ref, kept_ref)]
    copies = start_all(pairs, sems)
    piece = piece_ref.shape[0]
    start = pl.multiple_of(lax.axis_index("z") * piece, 8)
    piece_ref[...] = w_ref[lax.axis_index("x"), pl.ds(start, piece)]
    w_gate, w_up, w_down = parts(w_ref, units)
    pair = jnp.concatenate([own_ref[...], other_ref[...]], axis=0)
    in_sum, down_sum = weight_grad(
        split(jnp.concatenate([w_gate, w_up], axis=0)), split(w_down), [(pair[:, :width], pair[:, width:])]
    )
    out_ref[:, :units] = in_sum[:n].reshape(nx, units, width)
    out_ref[:, units : 2 * units] = in_sum[n:].reshape(nx, units, width)
    out_ref[:, 2 * units :] = down_sum.reshape(nx, units, width)
    for copy in copies:
        copy.wait()


def load_kernel(from_ref, to_ref, sems):
    n = to_ref.shape[0] // 2
    for copy in start_all([(from_ref.at[:n], to_ref.at[:n]), (from_ref.at[n:], to_ref.at[n:])], sems):
        copy.wait()


def outer_kernel(rows_ref, w_ref, out_ref, new_ref, sems):
    copies = start_all([(w_ref, new_ref)], sems)
    width = w_ref.shape[1]
    units = w_ref.shape[0] // 3
    step = 256
    chunks = [
        (rows_ref[at : at + step, :width], rows_ref[at : at + step, width:])
        for at in range(0, rows_ref.shape[0], step)
    ]
    in_sum, down_sum = weight_grad(split(w_ref[: 2 * units]), split(w_ref[2 * units :]), chunks)
    out_ref[: 2 * units] = in_sum
    out_ref[2 * units :] = down_sum
    copies[0].wait()


def query_grad(rows, cots, w_gate, w_up, w_down, up_way, down_way):
    rows, cots = split(rows), split(cots)
    gate, up_part = dot3(rows, w_gate, up_way), dot3(rows, w_up, up_way)
    hidden_grad = dot3(cots, w_down, NT)
    _, active, slope = gates(gate)
    return dot3(split(hidden_grad * up_part * slope), w_gate, down_way) + dot3(
        split(hidden_grad * active), w_up, down_way
    )


def zero_kernel(q_hbm_ref, c_hbm_ref, wg_hbm_ref, wu_hbm_ref, wd_hbm_ref, out_ref, *refs):
    *refs, sems = refs
    pairs = [(ref.at[0], to) for ref, to in zip((q_hbm_ref, c_hbm_ref, wg_hbm_ref, wu_hbm_ref, wd_hbm_ref), refs)]
    for copy in start_all(pairs, sems):
        copy.wait()
    q_ref, c_ref, wg_ref, wu_ref, wd_ref = refs
    out_ref[...] = query_grad(
        q_ref[...], c_ref[...], split(wg_ref[...]), split(wu_ref[...]), split(wd_ref[...]), NN, NT
    )


def one_kernel(q_ref, c_ref, w_ref, zero_ref, out_ref):
    w_gate, w_up, w_down = [split(w) for w in parts(w_ref, w_ref.shape[1] // 3)]
    out_ref[0] = zero_ref[...]
    out_ref[1] = query_grad(q_ref[...], c_ref[...], w_gate, w_up, w_down, NT, NN)


def prepare_kernel(
    pair_hbm_ref, w_hbm_ref, pair_ref, w_ref, gate_ref, up_ref, grad_ref, sems
):
    for copy in start_all([(pair_hbm_ref, pair_ref), (w_hbm_ref, w_ref)], sems):
        copy.wait()
    width = w_ref.shape[2]
    w_gate, w_up, w_down = [split(w) for w in parts(w_ref, w_ref.shape[1] // 3)]
    rows, cots = split(pair_ref[:, :width]), split(pair_ref[:, width:])
    gate_ref[...] = dot3(rows, w_gate, NT)
    up_ref[...] = dot3(rows, w_up, NT)
    grad_ref[...] = dot3(cots, w_down, NT)


def final_kernel(
    d_ref, pair_ref, w_ref, gate_ref, up_ref, grad_ref, new_ref, q_ref, c_ref, mine_ref, theirs_ref, new_out_ref, q_out_ref, c_out_ref, sems
):
    copies = start_all([(new_ref, new_out_ref), (q_ref.at[1], q_out_ref), (c_ref.at[1], c_out_ref)], sems)
    width = d_ref.shape[2]
    units = d_ref.shape[1] // 3
    d_gate, d_up, d_down = [split(d) for d in parts(d_ref, units)]
    w_gate, w_up, w_down = [split(w) for w in parts(w_ref, units)]
    rows, cots = split(pair_ref[:, :width]), split(pair_ref[:, width:])
    gate, up_part, hidden_grad = gate_ref[...], up_ref[...], grad_ref[...]
    sigma, active, slope = gates(gate)
    bend = sigma * (1.0 - sigma) * (2.0 + gate * (1.0 - 2.0 * sigma))
    steep = slope * up_part
    d_g, d_u = dot3(rows, d_gate, NT), dot3(rows, d_up, NT)
    d_c = dot3(cots, d_down, NT)
    d_h = steep * d_g + active * d_u
    value = dot3(split(active * up_part), d_down, NN) + dot3(split(d_h), w_down, NN)
    to_gate = hidden_grad * (up_part * bend * d_g + slope * d_u) + steep * d_c
    to_up = hidden_grad * slope * d_g + active * d_c
    key = (
        dot3(split(hidden_grad * steep), d_gate, NN)
        + dot3(split(hidden_grad * active), d_up, NN)
        + dot3(split(to_gate), w_gate, NN)
        + dot3(split(to_up), w_up, NN)
    )
    tok = mine_ref.shape[0]
    mine_ref[:, :width] = key[:tok]
    mine_ref[:, width:] = value[:tok]
    theirs_ref[:, :width] = key[tok:]
    theirs_ref[:, width:] = value[tok:]
    for copy in copies:
        copy.wait()


def join_kernel(scale, mine_ref, got_ref, rate_ref, k_ref, v_ref):
    width = k_ref.shape[1]
    k_ref[...] = scale * (mine_ref[:, :width] + got_ref[:, :width])
    rate = scale * rate_ref[...]
    for at in range(0, width, LANES):
        lanes = slice(width + at, width + at + LANES)
        v_ref[:, at : at + LANES] = rate * (mine_ref[:, lanes] + got_ref[:, lanes])


def after(value, *others):
    return lax.optimization_barrier((value, others))[0]


def both(*values):
    return lax.optimization_barrier(values)


def body(queries, keys, values, rates, grad_out, w_gate, w_up, w_down):
    tok, width = keys.shape
    hidden = w_gate.shape[2]
    n_z = lax.axis_size("z")
    units = hidden // (NX * NC)
    half = NX * units
    piece = 3 * units // n_z
    scale = float(tok * NX * NC * n_z) ** (-0.5)
    f32 = lambda *shape: jax.ShapeDtypeStruct(shape, jnp.float32)
    swap = lambda x: lax.ppermute(x, "c", [(i, (i + 1) % NC) for i in range(NC)])
    exchange = lambda x: lax.all_to_all(x.reshape(n_z, piece, width), "z", 0, 0)
    hold = lambda x: pltpu.with_memory_space_constraint(x, pltpu.HBM)
    n_mul = 2 * tok * width * half
    n_w = 12 * width * half
    here, there = pl.BlockSpec(memory_space=pltpu.VMEM), pl.BlockSpec(memory_space=pltpu.HBM)

    own, rate = call(
        pack_kernel,
        [f32(tok, 2 * width), f32(tok, LANES)],
        0,
        16 * tok * width,
        in_specs=[there] * 3,
        out_specs=[here] * 2,
        scratch_shapes=[
            pltpu.VMEM((tok, width), jnp.float32), pltpu.VMEM((1, tok), jnp.float32), pltpu.SemaphoreType.DMA((3,))
        ],
    )(hold(keys), hold(values), hold(rates.reshape(1, tok)))
    other = swap(own)
    w_rows, ask = call(
        units_kernel,
        [f32(NX, 3 * units, width), f32(tok, 2 * width)],
        0,
        2 * n_w,
        in_specs=[there] * 5,
        out_specs=[here] * 2,
        scratch_shapes=[pltpu.VMEM((2, width, half), jnp.float32), pltpu.SemaphoreType.DMA((4 + NX,))],
    )(*[hold(a) for a in (after(w_gate, own), w_up, w_down, queries, grad_out)])

    pair_shape = pltpu.HBM((2 * tok, 2 * width), jnp.float32)
    ask_shape = pltpu.HBM((tok, 2 * width), jnp.float32)
    kept_shape = pltpu.HBM((NX, 3 * units, width), jnp.float32)
    inner, w_piece, ask, pair, kept = call(
        inner_kernel,
        [f32(NX, 3 * units, width), f32(piece, width), ask_shape, pair_shape, kept_shape],
        36 * n_mul,
        2 * n_w,
        in_specs=[here] * 4,
        out_specs=[here, here, there, there, there],
        scratch_shapes=[pltpu.SemaphoreType.DMA((4,))],
    )(own, other, w_rows, ask)
    ask = lax.all_gather(ask, ("x", "c"), axis=0, tiled=True)
    inner = lax.all_to_all(inner, "x", 0, 0)
    inner = call(row_sum_kernel, f32(3 * units, width), 0, 2 * n_w)(inner)
    pieces = f32(n_z, piece, width)
    new = call(functools.partial(update_kernel, scale), pieces, 0, n_w)(exchange(inner), w_piece)
    ask = call(
        load_kernel,
        f32(*ask.shape),
        0,
        8 * ask.size,
        in_specs=[there],
        out_specs=here,
        scratch_shapes=[pltpu.SemaphoreType.DMA((2,))],
    )(hold(after(ask, new)))
    new, ask = both(exchange(new).reshape(3 * units, width), ask)

    outer, new = call(
        outer_kernel,
        [f32(3 * units, width), pltpu.HBM((3 * units, width), jnp.float32)],
        36 * n_mul,
        64 * tok * width,
        in_specs=[here, here],
        out_specs=[here, there],
        scratch_shapes=[pltpu.SemaphoreType.DMA((1,))],
    )(ask, new)
    new_all = lax.all_gather(new, ("x", "c"), axis=0, tiled=False)
    outer = call(total_kernel, pieces, 0, n_w)(exchange(outer))
    vmem = lambda *shape: pltpu.VMEM(shape, jnp.float32)
    zero = call(
        zero_kernel,
        f32(tok, width),
        30 * n_mul,
        2 * n_w,
        in_specs=[there] * 5,
        out_specs=here,
        scratch_shapes=[
            vmem(tok, width), vmem(tok, width), vmem(width, hidden), vmem(width, hidden), vmem(hidden, width),
            pltpu.SemaphoreType.DMA((5,)),
        ],
    )(*[hold(a) for a in (after(queries, outer), grad_out, w_gate, w_up, w_down)])
    loaded = call(
        prepare_kernel,
        [f32(2 * tok, 2 * width), f32(NX, 3 * units, width)] + [f32(2 * tok, half)] * 3,
        18 * n_mul,
        4 * n_w,
        in_specs=[there] * 2,
        out_specs=[here] * 5,
        scratch_shapes=[pltpu.SemaphoreType.DMA((2,))],
    )(hold(after(pair, zero)), hold(kept))
    outer, loaded = both(exchange(outer).reshape(3 * units, width), loaded)
    d_all, new_all = both(lax.all_gather(outer, "x", axis=0, tiled=False), new_all)
    mine, theirs, *ones = call(
        final_kernel,
        [f32(tok, 2 * width)] * 2 + [f32(*new_all.shape), f32(tok, width), f32(tok, width)],
        72 * n_mul,
        3 * n_w,
        in_specs=[here] * 6 + [there] * 3,
        out_specs=[here] * 5,
        scratch_shapes=[pltpu.SemaphoreType.DMA((3,))],
    )(d_all, *loaded, *[hold(a) for a in (new_all, queries, grad_out)])
    new_all, q_one, c_one = ones
    grad_queries = call(one_kernel, f32(2, tok, width), 30 * n_mul, 2 * n_w)(q_one, c_one, new_all, zero)
    theirs, grad_queries = both(swap(theirs), grad_queries)
    grad_keys, grad_values = call(
        functools.partial(join_kernel, scale), [f32(tok, width)] * 2, 0, 24 * tok * width
    )(mine, theirs, rate)
    return grad_queries, grad_keys, grad_values


def solution(mesh):
    devices = mesh.devices.reshape(-1, NX, NC, mesh.devices.shape[1])
    fine = Mesh(devices, ("z", "x", "c", "head"))
    ctx = ("z", "x", "c")
    in_specs = (
        P(None, ctx, "head"),
        P(ctx, "head"),
        P(ctx, "head"),
        P(ctx, "head"),
        P(None, ctx, "head"),
        P("head", None, None),
        P("head", None, None),
        P("head", None, None),
    )
    out_specs = (P(None, ctx, "head"), P(ctx, "head"), P(ctx, "head"))
    return jax.shard_map(body, mesh=fine, in_specs=in_specs, out_specs=out_specs, check_vma=False)
```

```python
import functools

import jax
import jax.numpy as jnp
from jax import lax
from jax.experimental import pallas as pl
from jax.experimental.pallas import tpu as pltpu
from jax.sharding import Mesh
from jax.sharding import PartitionSpec as P

NX, NC = 4, 2
NN = ((1,), (0,))
NT = ((1,), (1,))
MIB = 1 << 20
LANES = 128


def split(a):
    head = a.astype(jnp.bfloat16)
    tail = (a - head.astype(jnp.float32)).astype(jnp.bfloat16)
    return head, tail


def dot3(a, b, dims):
    rows = a[0].shape[0]
    dot = functools.partial(
        lax.dot_general, dimension_numbers=(dims, ((), ())), preferred_element_type=jnp.float32
    )
    both = dot(jnp.concatenate(a, axis=0), b[0])
    return both[:rows] + (both[rows:] + dot(a[0], b[1]))


def gates(gate):
    sigma = jax.nn.sigmoid(gate)
    return sigma, gate * sigma, sigma * (1.0 + gate * (1.0 - sigma))


def call(kernel, shapes, flops, n_bytes, limit=16, **more):
    return pl.pallas_call(
        kernel,
        out_shape=shapes,
        **more,
        compiler_params=pltpu.CompilerParams(vmem_limit_bytes=limit * MIB),
        cost_estimate=pl.CostEstimate(flops=flops, bytes_accessed=n_bytes, transcendentals=0),
    )


def start_all(pairs, sems):
    copies = [pltpu.make_async_copy(*pair, sems.at[i]) for i, pair in enumerate(pairs)]
    for copy in copies:
        copy.start()
    return copies


def pack_kernel(k_ref, v_ref, r_ref, inner_ref, rate_ref, raw_ref, row_ref, sems):
    width = k_ref.shape[1]
    tok = r_ref.shape[1]
    copies = start_all([(r_ref, row_ref), (v_ref, raw_ref), (k_ref, inner_ref.at[:, :width])], sems)
    copies[0].wait()
    rate = jnp.broadcast_to(row_ref[...], (LANES, tok)).T
    rate_ref[...] = rate
    copies[1].wait()
    for at in range(0, width, LANES):
        inner_ref[:, width + at : width + at + LANES] = rate * raw_ref[:, at : at + LANES]
    copies[2].wait()


def units_kernel(wg_ref, wu_ref, wd_ref, q_ref, c_ref, out_ref, ask_ref, raw_ref, sems):
    nx, rows, width = out_ref.shape
    units = rows // 3
    half = nx * units
    start = pl.multiple_of(lax.axis_index("c") * half, LANES)
    pairs = [
        (wg_ref.at[0, :, pl.ds(start, half)], raw_ref.at[0]),
        (wu_ref.at[0, :, pl.ds(start, half)], raw_ref.at[1]),
    ]
    pairs += [(wd_ref.at[0, pl.ds(start + i * units, units)], out_ref.at[i, 2 * units :]) for i in range(nx)]
    pairs += [(q_ref.at[1], ask_ref.at[:, :width]), (c_ref.at[1], ask_ref.at[:, width:])]
    copies = start_all(pairs, sems)
    for i in range(2):
        copies[i].wait()
        out_ref[:, i * units : (i + 1) * units] = raw_ref[i].T.reshape(nx, units, width)
    for copy in copies[2:]:
        copy.wait()


def row_sum_kernel(in_ref, out_ref):
    total = in_ref[0]
    for i in range(1, in_ref.shape[0]):
        total += in_ref[i]
    out_ref[...] = total


def update_kernel(scale, in_ref, w_ref, out_ref):
    n = in_ref.shape[0]
    total = in_ref[0]
    for i in range(1, n):
        total += in_ref[i]
    total = w_ref[...] + scale * total
    for i in range(n):
        out_ref[i] = total


def total_kernel(in_ref, out_ref):
    n = in_ref.shape[0]
    total = in_ref[0]
    for i in range(1, n):
        total += in_ref[i]
    for i in range(n):
        out_ref[i] = total


def parts(ref, units):
    width = ref.shape[2]
    return [ref[:, i * units : (i + 1) * units].reshape(-1, width) for i in range(3)]


def weight_grad(w_in, w_down, chunks):
    n = w_down[0].shape[0]
    total = None
    for rows, cots in chunks:
        rows, cots = split(rows), split(cots)
        both = dot3(w_in, rows, NT)
        hidden_grad = dot3(w_down, cots, NT)
        up_part = both[n:]
        _, active, slope = gates(both[:n])
        in_grad = jnp.concatenate([hidden_grad * up_part * slope, hidden_grad * active], axis=0)
        new = dot3(split(in_grad), rows, NN), dot3(split(active * up_part), cots, NN)
        total = new if total is None else (total[0] + new[0], total[1] + new[1])
    return total


def inner_kernel(own_ref, other_ref, w_ref, asked_ref, out_ref, piece_ref, ask_ref, pair_ref, kept_ref, sems):
    nx, rows, width = w_ref.shape
    units = rows // 3
    n = nx * units
    tok = own_ref.shape[0]
    pairs = [(asked_ref, ask_ref), (own_ref, pair_ref.at[:tok]), (other_ref, pair_ref.at[tok:]), (w_ref, kept_ref)]
    copies = start_all(pairs, sems)
    piece = piece_ref.shape[0]
    start = pl.multiple_of(lax.axis_index("z") * piece, 8)
    piece_ref[...] = w_ref[lax.axis_index("x"), pl.ds(start, piece)]
    w_gate, w_up, w_down = parts(w_ref, units)
    pair = jnp.concatenate([own_ref[...], other_ref[...]], axis=0)
    in_sum, down_sum = weight_grad(
        split(jnp.concatenate([w_gate, w_up], axis=0)), split(w_down), [(pair[:, :width], pair[:, width:])]
    )
    out_ref[:, :units] = in_sum[:n].reshape(nx, units, width)
    out_ref[:, units : 2 * units] = in_sum[n:].reshape(nx, units, width)
    out_ref[:, 2 * units :] = down_sum.reshape(nx, units, width)
    for copy in copies:
        copy.wait()


def load_kernel(from_ref, to_ref, sems):
    n = to_ref.shape[0] // 2
    for copy in start_all([(from_ref.at[:n], to_ref.at[:n]), (from_ref.at[n:], to_ref.at[n:])], sems):
        copy.wait()


def outer_kernel(rows_ref, w_ref, out_ref, new_ref, sems):
    copies = start_all([(w_ref, new_ref)], sems)
    width = w_ref.shape[1]
    units = w_ref.shape[0] // 3
    step = 256
    chunks = [
        (rows_ref[at : at + step, :width], rows_ref[at : at + step, width:])
        for at in range(0, rows_ref.shape[0], step)
    ]
    in_sum, down_sum = weight_grad(split(w_ref[: 2 * units]), split(w_ref[2 * units :]), chunks)
    out_ref[: 2 * units] = in_sum
    out_ref[2 * units :] = down_sum
    copies[0].wait()


def query_grad(rows, cots, w_gate, w_up, w_down, up_way, down_way):
    rows, cots = split(rows), split(cots)
    gate, up_part = dot3(rows, w_gate, up_way), dot3(rows, w_up, up_way)
    hidden_grad = dot3(cots, w_down, NT)
    _, active, slope = gates(gate)
    return dot3(split(hidden_grad * up_part * slope), w_gate, down_way) + dot3(
        split(hidden_grad * active), w_up, down_way
    )


def zero_kernel(q_hbm_ref, c_hbm_ref, wg_hbm_ref, wu_hbm_ref, wd_hbm_ref, out_ref, *refs):
    *refs, sems = refs
    pairs = [(ref.at[0], to) for ref, to in zip((q_hbm_ref, c_hbm_ref, wg_hbm_ref, wu_hbm_ref, wd_hbm_ref), refs)]
    for copy in start_all(pairs, sems):
        copy.wait()
    q_ref, c_ref, wg_ref, wu_ref, wd_ref = refs
    out_ref[...] = query_grad(
        q_ref[...], c_ref[...], split(wg_ref[...]), split(wu_ref[...]), split(wd_ref[...]), NN, NT
    )


def one_kernel(q_ref, c_ref, w_ref, zero_ref, out_ref, one_ref, sems):
    first = pltpu.make_async_copy(zero_ref, out_ref.at[0], sems.at[0])
    first.start()
    w_gate, w_up, w_down = [split(w) for w in parts(w_ref, w_ref.shape[1] // 3)]
    one_ref[...] = query_grad(q_ref[...], c_ref[...], w_gate, w_up, w_down, NT, NN)
    second = pltpu.make_async_copy(one_ref, out_ref.at[1], sems.at[1])
    second.start()
    first.wait()
    second.wait()


def prepare_kernel(
    pair_hbm_ref, w_hbm_ref, pair_ref, w_ref, gate_ref, up_ref, grad_ref, sems
):
    for copy in start_all([(pair_hbm_ref, pair_ref), (w_hbm_ref, w_ref)], sems):
        copy.wait()
    width = w_ref.shape[2]
    w_gate, w_up, w_down = [split(w) for w in parts(w_ref, w_ref.shape[1] // 3)]
    rows, cots = split(pair_ref[:, :width]), split(pair_ref[:, width:])
    gate_ref[...] = dot3(rows, w_gate, NT)
    up_ref[...] = dot3(rows, w_up, NT)
    grad_ref[...] = dot3(cots, w_down, NT)


def final_kernel(
    d_ref, pair_ref, w_ref, gate_ref, up_ref, grad_ref, new_ref, q_ref, c_ref, mine_ref, theirs_ref, new_out_ref, q_out_ref, c_out_ref, sems
):
    copies = start_all([(new_ref, new_out_ref), (q_ref.at[1], q_out_ref), (c_ref.at[1], c_out_ref)], sems)
    width = d_ref.shape[2]
    units = d_ref.shape[1] // 3
    d_gate, d_up, d_down = [split(d) for d in parts(d_ref, units)]
    w_gate, w_up, w_down = [split(w) for w in parts(w_ref, units)]
    rows, cots = split(pair_ref[:, :width]), split(pair_ref[:, width:])
    gate, up_part, hidden_grad = gate_ref[...], up_ref[...], grad_ref[...]
    sigma, active, slope = gates(gate)
    bend = sigma * (1.0 - sigma) * (2.0 + gate * (1.0 - 2.0 * sigma))
    steep = slope * up_part
    d_g, d_u = dot3(rows, d_gate, NT), dot3(rows, d_up, NT)
    d_c = dot3(cots, d_down, NT)
    d_h = steep * d_g + active * d_u
    value = dot3(split(active * up_part), d_down, NN) + dot3(split(d_h), w_down, NN)
    to_gate = hidden_grad * (up_part * bend * d_g + slope * d_u) + steep * d_c
    to_up = hidden_grad * slope * d_g + active * d_c
    key = (
        dot3(split(hidden_grad * steep), d_gate, NN)
        + dot3(split(hidden_grad * active), d_up, NN)
        + dot3(split(to_gate), w_gate, NN)
        + dot3(split(to_up), w_up, NN)
    )
    tok = mine_ref.shape[0]
    mine_ref[:, :width] = key[:tok]
    mine_ref[:, width:] = value[:tok]
    theirs_ref[:, :width] = key[tok:]
    theirs_ref[:, width:] = value[tok:]
    for copy in copies:
        copy.wait()


def join_kernel(scale, mine_ref, got_ref, rate_ref, k_ref, v_ref):
    width = k_ref.shape[1]
    k_ref[...] = scale * (mine_ref[:, :width] + got_ref[:, :width])
    rate = scale * rate_ref[...]
    for at in range(0, width, LANES):
        lanes = slice(width + at, width + at + LANES)
        v_ref[:, at : at + LANES] = rate * (mine_ref[:, lanes] + got_ref[:, lanes])


def after(value, *others):
    return lax.optimization_barrier((value, others))[0]


def both(*values):
    return lax.optimization_barrier(values)


def body(queries, keys, values, rates, grad_out, w_gate, w_up, w_down):
    tok, width = keys.shape
    hidden = w_gate.shape[2]
    n_z = lax.axis_size("z")
    units = hidden // (NX * NC)
    half = NX * units
    piece = 3 * units // n_z
    scale = float(tok * NX * NC * n_z) ** (-0.5)
    f32 = lambda *shape: jax.ShapeDtypeStruct(shape, jnp.float32)
    swap = lambda x: lax.ppermute(x, "c", [(i, (i + 1) % NC) for i in range(NC)])
    exchange = lambda x: lax.all_to_all(x.reshape(n_z, piece, width), "z", 0, 0)
    hold = lambda x: pltpu.with_memory_space_constraint(x, pltpu.HBM)
    n_mul = 2 * tok * width * half
    n_w = 12 * width * half
    here, there = pl.BlockSpec(memory_space=pltpu.VMEM), pl.BlockSpec(memory_space=pltpu.HBM)

    own, rate = call(
        pack_kernel,
        [f32(tok, 2 * width), f32(tok, LANES)],
        0,
        16 * tok * width,
        in_specs=[there] * 3,
        out_specs=[here] * 2,
        scratch_shapes=[
            pltpu.VMEM((tok, width), jnp.float32), pltpu.VMEM((1, tok), jnp.float32), pltpu.SemaphoreType.DMA((3,))
        ],
    )(hold(keys), hold(values), hold(rates.reshape(1, tok)))
    other = swap(own)
    w_rows, ask = call(
        units_kernel,
        [f32(NX, 3 * units, width), f32(tok, 2 * width)],
        0,
        2 * n_w,
        in_specs=[there] * 5,
        out_specs=[here] * 2,
        scratch_shapes=[pltpu.VMEM((2, width, half), jnp.float32), pltpu.SemaphoreType.DMA((4 + NX,))],
    )(*[hold(a) for a in (after(w_gate, own), w_up, w_down, queries, grad_out)])

    pair_shape = pltpu.HBM((2 * tok, 2 * width), jnp.float32)
    ask_shape = pltpu.HBM((tok, 2 * width), jnp.float32)
    kept_shape = pltpu.HBM((NX, 3 * units, width), jnp.float32)
    inner, w_piece, ask, pair, kept = call(
        inner_kernel,
        [f32(NX, 3 * units, width), f32(piece, width), ask_shape, pair_shape, kept_shape],
        36 * n_mul,
        2 * n_w,
        in_specs=[here] * 4,
        out_specs=[here, here, there, there, there],
        scratch_shapes=[pltpu.SemaphoreType.DMA((4,))],
    )(own, other, w_rows, ask)
    ask = lax.all_gather(ask, ("x", "c"), axis=0, tiled=True)
    inner = lax.all_to_all(inner, "x", 0, 0)
    inner = call(row_sum_kernel, f32(3 * units, width), 0, 2 * n_w)(inner)
    pieces = f32(n_z, piece, width)
    new = call(functools.partial(update_kernel, scale), pieces, 0, n_w)(exchange(inner), w_piece)
    ask = call(
        load_kernel,
        f32(*ask.shape),
        0,
        8 * ask.size,
        in_specs=[there],
        out_specs=here,
        scratch_shapes=[pltpu.SemaphoreType.DMA((2,))],
    )(hold(after(ask, new)))
    new, ask = both(exchange(new).reshape(3 * units, width), ask)

    outer, new = call(
        outer_kernel,
        [f32(3 * units, width), pltpu.HBM((3 * units, width), jnp.float32)],
        36 * n_mul,
        64 * tok * width,
        in_specs=[here, here],
        out_specs=[here, there],
        scratch_shapes=[pltpu.SemaphoreType.DMA((1,))],
    )(ask, new)
    new_all = lax.all_gather(new, ("x", "c"), axis=0, tiled=False)
    outer = call(total_kernel, pieces, 0, n_w)(exchange(outer))
    vmem = lambda *shape: pltpu.VMEM(shape, jnp.float32)
    zero = call(
        zero_kernel,
        f32(tok, width),
        30 * n_mul,
        2 * n_w,
        in_specs=[there] * 5,
        out_specs=here,
        scratch_shapes=[
            vmem(tok, width), vmem(tok, width), vmem(width, hidden), vmem(width, hidden), vmem(hidden, width),
            pltpu.SemaphoreType.DMA((5,)),
        ],
    )(*[hold(a) for a in (after(queries, outer), grad_out, w_gate, w_up, w_down)])
    loaded = call(
        prepare_kernel,
        [f32(2 * tok, 2 * width), f32(NX, 3 * units, width)] + [f32(2 * tok, half)] * 3,
        18 * n_mul,
        4 * n_w,
        in_specs=[there] * 2,
        out_specs=[here] * 5,
        scratch_shapes=[pltpu.SemaphoreType.DMA((2,))],
    )(hold(after(pair, zero)), hold(kept))
    outer, loaded = both(exchange(outer).reshape(3 * units, width), loaded)
    d_all, new_all = both(lax.all_gather(outer, "x", axis=0, tiled=False), new_all)
    mine, theirs, *ones = call(
        final_kernel,
        [f32(tok, 2 * width)] * 2 + [f32(*new_all.shape), f32(tok, width), f32(tok, width)],
        72 * n_mul,
        3 * n_w,
        in_specs=[here] * 6 + [there] * 3,
        out_specs=[here] * 5,
        scratch_shapes=[pltpu.SemaphoreType.DMA((3,))],
    )(d_all, *loaded, *[hold(a) for a in (new_all, queries, grad_out)])
    new_all, q_one, c_one = ones
    grad_queries = call(
        one_kernel,
        pltpu.HBM((2, tok, width), jnp.float32),
        30 * n_mul,
        2 * n_w,
        in_specs=[here] * 4,
        out_specs=there,
        scratch_shapes=[vmem(tok, width), pltpu.SemaphoreType.DMA((2,))],
    )(q_one, c_one, new_all, zero)
    theirs, grad_queries = both(swap(theirs), grad_queries)
    grad_keys, grad_values = call(
        functools.partial(join_kernel, scale), [f32(tok, width)] * 2, 0, 24 * tok * width
    )(mine, theirs, rate)
    return grad_queries, grad_keys, grad_values


def solution(mesh):
    devices = mesh.devices.reshape(-1, NX, NC, mesh.devices.shape[1])
    fine = Mesh(devices, ("z", "x", "c", "head"))
    ctx = ("z", "x", "c")
    in_specs = (
        P(None, ctx, "head"),
        P(ctx, "head"),
        P(ctx, "head"),
        P(ctx, "head"),
        P(None, ctx, "head"),
        P("head", None, None),
        P("head", None, None),
        P("head", None, None),
    )
    out_specs = (P(None, ctx, "head"), P(ctx, "head"), P(ctx, "head"))
    return jax.shard_map(body, mesh=fine, in_specs=in_specs, out_specs=out_specs, check_vma=False)
```
